32 devices in a mesh: groups: 2 (over x), seq: 16 (over z, y, core).
Axes of the slice: x: 2, y: 2, z: 4, core: 2. Of those that a mesh axis runs over, the one named last changes fastest.
Arguments:
- queries: bfloat16 [8192, 768], P(('groups', 'seq')), parts along dimension 0, may hold values from -10 to 10
- keys: bfloat16 [8192, 768], P(('groups', 'seq')), parts along dimension 0, may hold values from -10 to 10
- values: bfloat16 [8192, 768], P(('groups', 'seq')), parts along dimension 0, may hold values from -6 to 6
- grad_out: bfloat16 [8192, 768], P(('groups', 'seq')), parts along dimension 0, may hold values from -6 to 6
- local_span: int32 [16], replicated, may hold values from 64 to 256, as said below
- head_residue: int32 [16], replicated, may hold values from 0 to 15
- valid_count: int32 [2], P('groups'), parts along dimension 0, may hold values from 1024 to 4096
Outputs:
- query_gradient: bfloat16 [8192, 768], P(('groups', 'seq')), parts along dimension 0
- key_gradient: bfloat16 [8192, 768], P(('groups', 'seq')), parts along dimension 0
- value_gradient: bfloat16 [8192, 768], P(('groups', 'seq')), parts along dimension 0
The draws below stay inside these ranges and needn't reach their ends.
There are 2 independent parts, one for each index of `groups`. The reference program is written for one: setup_inputs(seed, part) draws one part's arguments, and reference() takes and returns one part's arrays. A program takes and returns all parts, laid end to end along the dimension named above; an argument that names none is the same for every part. Nothing has to cross between parts.
Inputs may be any that keep to these rules, and one draw needn't show every extreme that they name: `local_span`: each head's local segment length is 256, 128 or 64; the longest and the shortest both occur. Positions from valid_count on are padding tiles.
All inputs are finite; a program needn't handle non-finite values.
Results may differ from the reference program's by a relative error of at most 0.0072.
Values may be sent and summed in bfloat16 or wider, within the bound.
A program may use at most 128 MiB of HBM per device.

```python
import math
import jax
import jax.numpy as jnp
from jax import lax

HEADS = 16
HEAD_DIM = 48
DILATION_STEP = 16
PARTS_IN_WINDOW = 16
TOKENS_PER_SHARD = 256
WIDTH = 768
SEQ_LEN = 4096


def paired_rows(key):
    base = jax.random.fold_in(key, 11)
    key_query, key_key = jax.random.split(base, 2)
    queries_all = jnp.clip(jax.random.normal(key_query, (SEQ_LEN, WIDTH), jnp.float32), -6.0, 6.0)
    keys_all = jnp.clip(jax.random.normal(key_key, (SEQ_LEN, WIDTH), jnp.float32), -6.0, 6.0)
    return (queries_all, keys_all)


def draw_queries(key, part):
    return paired_rows(key)[0].astype(jnp.bfloat16)


def draw_keys(key, part):
    return paired_rows(key)[1].astype(jnp.bfloat16)


def draw_local_span(key, part):
    key_level, key_order = jax.random.split(jax.random.fold_in(key, 3))
    levels = jax.random.randint(key_level, (HEADS,), 0, 3)
    order = jax.random.permutation(key_order, HEADS)
    levels = levels.at[order[0]].set(0).at[order[1]].set(2)
    spans = jnp.where(levels == 0, TOKENS_PER_SHARD, jnp.where(levels == 1, TOKENS_PER_SHARD // 2, TOKENS_PER_SHARD // 4))
    return spans.astype(jnp.int32)


def with_ends(values, stream_key, smallest, largest):
    shape = values.shape
    index_at = [jax.random.randint(jax.random.fold_in(stream_key, axis), (), 0, shape[axis]) for axis in range(len(shape))]
    values = values.at[tuple(index_at)].set(smallest)
    longest = shape.index(max(shape))
    index_at[longest] = (index_at[longest] + 1) % shape[longest]
    return values.at[tuple(index_at)].set(largest)


def block_levels(rng, extent, cuts, low, top_value):
    level = 1.0
    for axis_at, parts in cuts:
        heights = jax.random.uniform(jax.random.fold_in(jax.random.fold_in(rng, 6), axis_at), (parts,), jnp.float32, low / len(cuts), top_value / len(cuts))
        level = level * jnp.repeat(jnp.exp(heights), extent[axis_at] // parts).reshape((-1,) + (1,) * (len(extent) - 1 - axis_at))
    return level


def gaussian(rng, dims, width, most, shards=(), kind=jnp.bfloat16):
    values = width * jax.random.normal(rng, dims, jnp.float32)
    if shards:
        values = values * block_levels(rng, dims, shards, -0.22, 0.18)
    return jnp.clip(values, -most, most).astype(kind)


def setup_inputs(seed: int = 0, part: int = 0) -> dict:
    streams_of = jax.random.split(jax.random.key(seed), 8)
    own_keys = jax.random.split(jax.random.fold_in(streams_of[7], part), 8)
    queries = draw_queries(jax.random.fold_in(jax.random.fold_in(streams_of[7], part), 71), part)
    keys = draw_keys(jax.random.fold_in(jax.random.fold_in(streams_of[7], part), 71), part)
    values = gaussian(own_keys[2], (SEQ_LEN, WIDTH), 1.0, 6.0, ((0, 16),))
    grad_out = gaussian(own_keys[3], (SEQ_LEN, WIDTH), 1.0, 6.0, ((0, 16),))
    local_span = draw_local_span(jax.random.fold_in(streams_of[7], 71), part)
    head_residue = with_ends(jax.random.randint(streams_of[5], (HEADS,), 0, DILATION_STEP), jax.random.fold_in(streams_of[5], 1), 0, DILATION_STEP - 1).astype(jnp.int32)
    valid_count = jax.random.randint(own_keys[6], (1,), SEQ_LEN // 4, SEQ_LEN + 1).astype(jnp.int32)
    return dict(queries=queries, keys=keys, values=values, grad_out=grad_out, local_span=local_span, head_residue=head_residue, valid_count=valid_count)


SCORE_FLOOR = -1e+30
PRECISE_MODE = lax.Precision.HIGHEST

def select_heads(tokens_heads, indicator_matrix):
    grouped = tokens_heads.reshape(tokens_heads.shape[0] // DILATION_STEP, DILATION_STEP, tokens_heads.shape[1], tokens_heads.shape[2])
    return jnp.einsum('trhe,hr->the', grouped, indicator_matrix, precision=PRECISE_MODE)

def select_statistics(stats, indicator_matrix):
    grouped = stats.reshape(stats.shape[0] // DILATION_STEP, DILATION_STEP, stats.shape[1])
    return jnp.einsum('trh,hr->th', grouped, indicator_matrix, precision=PRECISE_MODE)

def distribute_heads(picked, indicator_matrix):
    full_rows = jnp.einsum('the,hr->trhe', picked, indicator_matrix, precision=PRECISE_MODE)
    return full_rows.reshape(-1, picked.shape[1], picked.shape[2])

def distribute_statistics(picked, indicator_matrix):
    full_rows = jnp.einsum('th,hr->trh', picked, indicator_matrix, precision=PRECISE_MODE)
    return full_rows.reshape(-1, picked.shape[1])

def round_half(values_f):
    return lax.optimization_barrier(values_f.astype(jnp.bfloat16)).astype(jnp.float32)

def reference(queries, keys, values, grad_out, local_span, head_residue, valid_count):
    sequence_rows = queries.shape[0]
    hidden_width = queries.shape[1]
    score_scale = 1.0 / math.sqrt(HEAD_DIM)
    mask_count_total = valid_count[0]
    query_complete = queries.astype(jnp.float32).reshape(sequence_rows, HEADS, HEAD_DIM)
    key_complete = keys.astype(jnp.float32).reshape(sequence_rows, HEADS, HEAD_DIM)
    value_complete = values.astype(jnp.float32).reshape(sequence_rows, HEADS, HEAD_DIM)
    gradient_bundle = grad_out.astype(jnp.float32).reshape(sequence_rows, HEADS, HEAD_DIM)
    indicator_matrix = (head_residue[:, None] == jnp.arange(DILATION_STEP, dtype=jnp.int32)[None, :]).astype(jnp.float32)
    positions = jnp.arange(sequence_rows, dtype=jnp.int32)
    row_mask = positions < mask_count_total
    block_count = sequence_rows // TOKENS_PER_SHARD

    def blocked(array):
        return array.reshape((block_count, TOKENS_PER_SHARD) + array.shape[1:])
    inner = jnp.arange(TOKENS_PER_SHARD, dtype=jnp.int32)
    segment_of = inner[None, :] // local_span[:, None]
    same_local = segment_of[:, :, None] == segment_of[:, None, :]

    def local_scores(query_blk, key_blk):
        return jnp.einsum('ihe,jhe->hij', query_blk, key_blk, precision=PRECISE_MODE) * score_scale

    def local_stats(operands):
        query_blk, key_blk, valid_blk = operands
        scores = local_scores(query_blk, key_blk)
        allowed = same_local & valid_blk[None, None, :]
        running_maximum = lax.optimization_barrier(jnp.max(jnp.where(allowed, scores, SCORE_FLOOR), axis=2))
        row_count_total = lax.optimization_barrier(jnp.sum(jnp.where(allowed, jnp.exp(scores - running_maximum[:, :, None]), 0.0), axis=2))
        return jnp.transpose(running_maximum + jnp.log(row_count_total + 1.0 - valid_blk.astype(jnp.float32)[None, :]))
    dense_logsumexp = lax.map(local_stats, (blocked(query_complete), blocked(key_complete), blocked(row_mask)))
    dense_logsumexp = dense_logsumexp.reshape(sequence_rows, HEADS)
    thinned_probes = select_heads(query_complete, indicator_matrix)
    sparse_keys = select_heads(key_complete, indicator_matrix)
    sparse_values = select_heads(value_complete, indicator_matrix)
    sparse_output_gradient = select_heads(gradient_bundle, indicator_matrix)
    sparse_positions = jnp.arange(sequence_rows // DILATION_STEP, dtype=jnp.int32)[:, None] * DILATION_STEP + head_residue[None, :]
    sparse_row_mask = sparse_positions < mask_count_total
    sparse_segment = sparse_positions // (PARTS_IN_WINDOW * TOKENS_PER_SHARD)
    dense_sparse_logsumexp = select_statistics(dense_logsumexp, indicator_matrix)

    def head_split(array):
        return jnp.swapaxes(array, 0, 1)

    def sparse_branch_forward(operands):
        query_h, key_h, value_h, head_mask, segment_h, dense_head_output = operands
        scores = jnp.dot(query_h, key_h.T, precision=PRECISE_MODE) * score_scale
        allowed = (segment_h[:, None] == segment_h[None, :]) & head_mask[None, :]
        running_maximum = lax.optimization_barrier(jnp.max(jnp.where(allowed, scores, SCORE_FLOOR), axis=1))
        row_count_total = lax.optimization_barrier(jnp.sum(jnp.where(allowed, jnp.exp(scores - running_maximum[:, None]), 0.0), axis=1))
        sparse_logsumexp = running_maximum + jnp.log(row_count_total + 1.0 - head_mask.astype(jnp.float32))
        merged_output = jnp.where(head_mask, jnp.logaddexp(dense_head_output, sparse_logsumexp), 0.0)
        weight = jnp.where(allowed & head_mask[:, None], jnp.exp(scores - merged_output[:, None]), 0.0)
        return (merged_output, jnp.dot(weight, value_h, precision=PRECISE_MODE))
    merged_head_output, sparse_head_output = lax.map(sparse_branch_forward, (head_split(thinned_probes), head_split(sparse_keys), head_split(sparse_values), sparse_row_mask.T, sparse_segment.T, dense_sparse_logsumexp.T))
    merged_output = merged_head_output.T
    global_output = distribute_heads(head_split(sparse_head_output), indicator_matrix)
    complete_logsumexp = jnp.where(row_mask[:, None], dense_logsumexp + distribute_statistics(merged_output - dense_sparse_logsumexp, indicator_matrix), 0.0)

    def local_backward(operands):
        query_blk, key_blk, value_blk, grad_blk, lse_blk, glob_blk, valid_blk = operands
        scores = local_scores(query_blk, key_blk)
        allowed = same_local & valid_blk[None, None, :] & valid_blk[None, :, None]
        weight = jnp.where(allowed, jnp.exp(scores - jnp.transpose(lse_blk)[:, :, None]), 0.0)
        weight_half = round_half(weight)
        output = jnp.einsum('hij,jhe->ihe', weight_half, value_blk, precision=PRECISE_MODE) + glob_blk
        delta_blk = jnp.where(valid_blk[:, None], lax.optimization_barrier(jnp.sum(grad_blk * output, axis=2)), 0.0)
        grad_value = jnp.einsum('hij,ihe->jhe', weight_half, grad_blk, precision=PRECISE_MODE)
        dprod = jnp.einsum('ihe,jhe->hij', grad_blk, value_blk, precision=PRECISE_MODE)
        logit_derivative = round_half(weight * (dprod - jnp.transpose(delta_blk)[:, :, None]))
        grad_query = score_scale * jnp.einsum('hij,jhe->ihe', logit_derivative, key_blk, precision=PRECISE_MODE)
        grad_key = score_scale * jnp.einsum('hij,ihe->jhe', logit_derivative, query_blk, precision=PRECISE_MODE)
        return (grad_query, grad_key, grad_value, delta_blk)
    dense_query_gradient, dense_key_gradient, dense_value_gradient, row_delta = lax.map(local_backward, (blocked(query_complete), blocked(key_complete), blocked(value_complete), blocked(gradient_bundle), blocked(complete_logsumexp), blocked(global_output), blocked(row_mask)))
    shape_full = (sequence_rows, HEADS, HEAD_DIM)
    dense_query_gradient = dense_query_gradient.reshape(shape_full)
    dense_key_gradient = dense_key_gradient.reshape(shape_full)
    dense_value_gradient = dense_value_gradient.reshape(shape_full)
    row_delta = row_delta.reshape(sequence_rows, HEADS)
    sparse_row_delta = select_statistics(row_delta, indicator_matrix)

    def sparse_branch_backward(operands):
        query_h, key_h, value_h, grad_h, head_mask, segment_h, combined_row, delta_row = operands
        scores = jnp.dot(query_h, key_h.T, precision=PRECISE_MODE) * score_scale
        allowed = (segment_h[:, None] == segment_h[None, :]) & head_mask[None, :] & head_mask[:, None]
        weight = jnp.where(allowed, jnp.exp(scores - combined_row[:, None]), 0.0)
        weight_half = round_half(weight)
        grad_value = jnp.dot(weight_half.T, grad_h, precision=PRECISE_MODE)
        dprod = jnp.dot(grad_h, value_h.T, precision=PRECISE_MODE)
        logit_derivative = round_half(weight * (dprod - delta_row[:, None]))
        grad_query = score_scale * jnp.dot(logit_derivative, key_h, precision=PRECISE_MODE)
        grad_key = score_scale * jnp.dot(logit_derivative.T, query_h, precision=PRECISE_MODE)
        return (grad_query, grad_key, grad_value)
    sparse_query_gradient, sparse_key_gradient, sparse_value_gradient = lax.map(sparse_branch_backward, (head_split(thinned_probes), head_split(sparse_keys), head_split(sparse_values), head_split(sparse_output_gradient), sparse_row_mask.T, sparse_segment.T, merged_output.T, sparse_row_delta.T))
    query_gradient = (dense_query_gradient + distribute_heads(head_split(sparse_query_gradient), indicator_matrix)).astype(jnp.bfloat16).reshape(sequence_rows, hidden_width)
    key_gradient = (dense_key_gradient + distribute_heads(head_split(sparse_key_gradient), indicator_matrix)).astype(jnp.bfloat16).reshape(sequence_rows, hidden_width)
    value_gradient = (dense_value_gradient + distribute_heads(head_split(sparse_value_gradient), indicator_matrix)).astype(jnp.bfloat16).reshape(sequence_rows, hidden_width)
    return (query_gradient, key_gradient, value_gradient)
```

```python
import math

import jax
import jax.numpy as jnp
from jax import lax
from jax.experimental import pallas as pl
from jax.experimental.pallas import tpu as pltpu
from jax.sharding import PartitionSpec as P

STEP = 16
WINDOW = 16
ORDER = tuple(range(WINDOW - 1, 0, -1))
FLOOR = -1e30
LOG2E = 1.4426950408889634
EARLY_HEADS = 8
VMEM_LIMIT = 63 * 2**20

BF = jnp.bfloat16
F32 = jnp.float32


def nn(a, b):
    return lax.dot_general(a, b, (((1,), (0,)), ((), ())), preferred_element_type=F32)


def nt(a, b):
    return lax.dot_general(a, b, (((1,), (1,)), ((), ())), preferred_element_type=F32)


def tn(a, b):
    return lax.dot_general(a, b, (((0,), (0,)), ((), ())), preferred_element_type=F32)


def parts_of(x, count):
    out = []
    for _ in range(count - 1):
        head = x.astype(BF).astype(F32)
        out.append(head)
        x = x - head
    out.append(x)
    return out


def rows_block(rows, height, width):
    at = lax.broadcasted_iota(jnp.int32, (height, width), 0)
    block = jnp.zeros((height, width), F32)
    for n, row in enumerate(rows):
        block = jnp.where(at == n, row, block)
    return block


def kernel(
    span_ref, res_ref, count_hbm, q_hbm, k_hbm, v_hbm, g_hbm,
    dq_hbm, dk_hbm, dv_hbm,
    dq_ref, dk_ref, dv_ref, store_sem, q_ref, k_ref, v_ref, g_ref, load_sem, qt, kt, vt, gt, dqt, dkt, dvt, qb, gb, pick, far, pb, dpb,
    send1, recv1, send2, recv2, ss1, rs1, ss2, rs2, count_ref, count_sem,
):
    tokens, width = q_ref.shape
    heads = span_ref.shape[0]
    dim = width // heads
    few = tokens // STEP
    chosen = heads * few
    scale = 1.0 / math.sqrt(dim)
    scale2 = scale * LOG2E
    me = lax.axis_index("seq")
    base = (me // WINDOW) * WINDOW
    my = me - base
    count_copy = pltpu.make_async_copy(count_hbm, count_ref, count_sem)
    count_copy.start()
    loads = [
        pltpu.make_async_copy(source, target, load_sem.at[n])
        for n, (source, target) in enumerate(
            ((q_hbm, q_ref), (g_hbm, g_ref), (k_hbm, k_ref), (v_hbm, v_ref))
        )
    ]
    for load in loads:
        load.start()

    bits = [lax.rem(my // b, 2) for b in (1, 2, 4, 8)]

    def partner(n):
        to = my
        for at, b in enumerate((1, 2, 4, 8)):
            if n & b:
                to = to + b - 2 * b * bits[at]
        return to

    barrier = pltpu.get_barrier_semaphore()

    for n in ORDER:
        pl.semaphore_signal(
            barrier, inc=1, device_id={"seq": base + partner(n)},
            device_id_type=pl.DeviceIdType.MESH,
        )

    def block_of(n):
        return pl.ds(pl.multiple_of(n * few, few), few)

    def exchange(n, source, target, send_sem, recv_sem):
        to = partner(n)
        return pltpu.make_async_remote_copy(
            src_ref=source.at[block_of(to)],
            dst_ref=target.at[block_of(my)],
            send_sem=send_sem.at[n],
            recv_sem=recv_sem.at[n],
            device_id={"seq": base + to},
            device_id_type=pl.DeviceIdType.MESH,
        )

    def start_all(*args):
        for n in ORDER:
            exchange(n, *args).start()

    def wait_all(*args):
        for n in ORDER[::-1]:
            exchange(n, *args).wait_recv()

    def wait_sent(*args):
        for n in ORDER:
            exchange(n, *args).wait_send()

    count_copy.wait()
    count = count_ref[0]
    lane = lax.broadcasted_iota(jnp.int32, (1, chosen), 1)
    lane_head = lane // few
    lane_res = jnp.zeros((1, chosen), jnp.int32)
    lane_span = jnp.zeros((1, chosen), jnp.int32)
    for h in range(heads):
        lane_res = jnp.where(lane_head == h, res_ref[h], lane_res)
        lane_span = jnp.where(lane_head == h, span_ref[h], lane_span)
    lane_token = (lane % few) * STEP + lane_res
    row = lax.broadcasted_iota(jnp.int32, (tokens, tokens), 0)
    col = lax.broadcasted_iota(jnp.int32, (tokens, tokens), 1)
    start = me * tokens
    huge = jnp.int32(1 << 20)
    row_ok = row + start < count
    far[...] = jnp.where(row_ok, row ^ col, huge)
    pick[...] = (row == lane_token).astype(F32).astype(BF)

    for load, source, target in zip(
        loads, (q_ref, g_ref, k_ref, v_ref), (qt, gt, kt, vt)
    ):
        load.wait()
        target[...] = source[...].T

    def picked(source, keep):
        full = nn(source[...], pick[...])
        total = jnp.zeros((dim, chosen), F32)
        for h in range(heads):
            part = jnp.where(lane_head == h, full[h * dim : (h + 1) * dim], 0.0)
            if keep is not None:
                keep[h * dim : (h + 1) * dim, :] = part.astype(BF)
            total = total + part
        return total

    q_few = picked(qt, qb)
    g_few = picked(gt, gb)
    k_few = picked(kt, None)
    v_few = picked(vt, None)

    mask = jnp.where(row_ok, row ^ lane_token, huge) < lane_span
    s = jnp.where(mask, nn(k_ref[...], qb[...]) * scale2, FLOOR)
    top = jnp.max(s, axis=0, keepdims=True)
    p = jnp.exp2(s - top)
    total = jnp.sum(p, axis=0, keepdims=True)
    p = p * (1.0 / total)
    dp = nn(v_ref[...], gb[...])
    local_lse = top + jnp.log(total) * LOG2E
    local_delta = jnp.sum(p * dp, axis=0, keepdims=True)
    pb[...] = p
    dpb[...] = dp
    tail = chosen - 4 * dim
    stats = rows_block(parts_of(local_lse, 3) + parts_of(local_delta, 2), tail, chosen)
    packed = jnp.concatenate([q_few, k_few, v_few, g_few, stats], axis=0)
    send1[...] = packed.T.astype(BF)

    pl.semaphore_wait(barrier, WINDOW - 1)
    start_all(send1, recv1, ss1, rs1)
    recv1[block_of(my), :] = send1[block_of(my), :]

    query_ok = lane + start < count

    def local_head(h, carry):
        at = pl.ds(pl.multiple_of(h * dim, 16), dim)
        qh, kh, vh, gh = qt[at, :], kt[at, :], vt[at, :], gt[at, :]
        s = jnp.where(far[...] < span_ref[h], tn(kh, qh) * scale2, FLOOR)
        top = jnp.max(s, axis=0, keepdims=True)
        p = jnp.exp2(s - top)
        inverse = 1.0 / jnp.sum(p, axis=0, keepdims=True)
        dp = tn(vh, gh)
        delta = jnp.sum(p * dp, axis=0, keepdims=True) * inverse
        keep = query_ok & (lane % STEP != res_ref[h])
        w = p * jnp.where(keep, inverse, 0.0)
        ds = (w * (dp - delta)).astype(BF)
        dqt[at, :] = nn(kh, ds) * scale
        dkt[at, :] = nt(qh, ds) * scale
        dvt[at, :] = nt(gh, w.astype(BF))
        return carry

    lax.fori_loop(0, EARLY_HEADS, local_head, 0, unroll=4)

    wait_all(send1, recv1, ss1, rs1)
    got = recv1[...].astype(F32).T
    got_half = got.astype(BF)
    qh, kh = got_half[0:dim], got_half[dim : 2 * dim]
    vh, gh = got_half[2 * dim : 3 * dim], got_half[3 * dim : 4 * dim]
    at = 4 * dim
    local_lse = got[at : at + 1] + got[at + 1 : at + 2] + got[at + 2 : at + 3]
    local_delta = got[at + 3 : at + 4] + got[at + 4 : at + 5]
    limit = count - base * tokens - res_ref[my]
    s = jnp.where(row * STEP < limit, tn(kh, qh) * scale2, FLOOR)
    top = jnp.max(s, axis=0, keepdims=True)
    p = jnp.exp2(s - top)
    total = jnp.sum(p, axis=0, keepdims=True)
    dilated_lse = top + jnp.log(total) * LOG2E
    most = jnp.maximum(local_lse, dilated_lse)
    both = most + jnp.log(jnp.exp2(local_lse - most) + jnp.exp2(dilated_lse - most)) * LOG2E
    here_ok = lane * STEP < limit
    local_part = jnp.where(here_ok, jnp.exp2(local_lse - both), 0.0)
    u = p * jnp.where(here_ok, jnp.exp2(top - both), 0.0)
    dp = tn(vh, gh)
    delta = local_part * local_delta + jnp.sum(u * dp, axis=0, keepdims=True)
    delta = jnp.where(here_ok, delta, 0.0)
    ds = (u * (dp - delta)).astype(BF)
    stats = rows_block(parts_of(local_part, 2) + parts_of(delta, 2), chosen - 3 * dim, chosen)
    packed = jnp.concatenate(
        [nn(kh, ds) * scale, nt(qh, ds) * scale, nt(gh, u.astype(BF)), stats], axis=0
    )
    send2[...] = packed.T.astype(BF)
    start_all(send2, recv2, ss2, rs2)
    recv2[block_of(my), :] = send2[block_of(my), :]

    lax.fori_loop(EARLY_HEADS, heads, local_head, 0, unroll=4)

    wait_all(send2, recv2, ss2, rs2)
    back = recv2[...].astype(F32).T
    at = 3 * dim
    local_part = back[at : at + 1] + back[at + 1 : at + 2]
    delta = back[at + 2 : at + 3] + back[at + 3 : at + 4]
    w = pb[...] * local_part
    ds = (w * (dpb[...] - delta)).astype(BF)
    wide = nn(kt[...], ds) * scale
    dq_few, dk_few, dv_few = back[0:dim], back[dim : 2 * dim], back[2 * dim : 3 * dim]

    def spread(piece_of):
        pieces = [
            jnp.where(lane_head == h, piece_of(h), 0.0).astype(BF) for h in range(heads)
        ]
        return nt(jnp.concatenate(pieces, axis=0), pick[...])

    def store(n, source, target):
        copy = pltpu.make_async_copy(source, target, store_sem.at[n])
        copy.start()
        return copy

    dq = dqt[...] + spread(lambda h: wide[h * dim : (h + 1) * dim] + dq_few)
    dq_ref[...] = dq.astype(BF)
    store_dq = store(0, dq_ref, dq_hbm)
    dk = dkt[...] + nt(qb[...], ds) * scale + spread(lambda h: dk_few)
    dk_ref[...] = dk.astype(BF)
    store_dk = store(1, dk_ref, dk_hbm)
    dv = dvt[...] + nt(gb[...], w.astype(BF)) + spread(lambda h: dv_few)
    dv_ref[...] = dv.astype(BF)
    store_dv = store(2, dv_ref, dv_hbm)
    wait_sent(send1, recv1, ss1, rs1)
    wait_sent(send2, recv2, ss2, rs2)
    store_dq.wait()
    store_dk.wait()
    store_dv.wait()


def finish(a_in, b_in, c_in, a_out, b_out, c_out, sources, targets, load_sem, store_sem):
    loads = [
        pltpu.make_async_copy(ref, sources.at[n], load_sem.at[n])
        for n, ref in enumerate((a_in, b_in, c_in))
    ]
    for load in loads:
        load.start()
    stores = [
        pltpu.make_async_copy(targets.at[n], ref, store_sem.at[n])
        for n, ref in enumerate((a_out, b_out, c_out))
    ]
    for n in range(3):
        loads[n].wait()
        targets[n] = sources[n].T
        stores[n].start()
    for store in stores:
        store.wait()


def shards(queries, keys, values, grad_out, local_span, head_residue, valid_count):
    tokens, width = queries.shape
    heads = local_span.shape[0]
    chosen = heads * (tokens // STEP)
    assert heads == WINDOW and chosen == tokens
    smem = pl.BlockSpec(memory_space=pltpu.SMEM)
    vmem = pl.BlockSpec(memory_space=pltpu.VMEM)
    hbm = pl.BlockSpec(memory_space=pltpu.MemorySpace.HBM)
    out = jax.ShapeDtypeStruct((tokens, width), BF)
    turned = jax.ShapeDtypeStruct((width, tokens), BF)
    gradients = pl.pallas_call(
        kernel,
        out_shape=(turned, turned, turned),
        in_specs=[smem] * 2 + [hbm] * 5,
        out_specs=(hbm, hbm, hbm),
        scratch_shapes=[pltpu.VMEM((width, tokens), BF)] * 3
        + [pltpu.SemaphoreType.DMA((3,))]
        + [pltpu.VMEM((tokens, width), BF)] * 4
        + [pltpu.SemaphoreType.DMA((4,))]
        + [pltpu.VMEM((width, tokens), BF)] * 4
        + [pltpu.VMEM((width, tokens), F32)] * 3
        + [pltpu.VMEM((width, chosen), BF)] * 2
        + [
            pltpu.VMEM((tokens, chosen), BF),
            pltpu.VMEM((tokens, tokens), jnp.int32),
            pltpu.VMEM((tokens, chosen), F32),
            pltpu.VMEM((tokens, chosen), F32),
        ]
        + [pltpu.VMEM((chosen, chosen), BF)] * 4
        + [pltpu.SemaphoreType.DMA((WINDOW,))] * 4
        + [pltpu.SMEM((1,), jnp.int32), pltpu.SemaphoreType.DMA],
        compiler_params=pltpu.CompilerParams(
            collective_id=0, has_side_effects=True, vmem_limit_bytes=VMEM_LIMIT
        ),
    )(local_span, head_residue, valid_count, queries, keys, values, grad_out)
    return pl.pallas_call(
        finish,
        out_shape=(out, out, out),
        in_specs=[hbm] * 3,
        out_specs=(hbm, hbm, hbm),
        scratch_shapes=[
            pltpu.VMEM((3, width, tokens), BF),
            pltpu.VMEM((3, tokens, width), BF),
            pltpu.SemaphoreType.DMA((3,)),
            pltpu.SemaphoreType.DMA((3,)),
        ],
        compiler_params=pltpu.CompilerParams(vmem_limit_bytes=VMEM_LIMIT),
    )(*gradients)


def solution(mesh):
    rows = P(("groups", "seq"), None)
    return jax.shard_map(
        shards,
        mesh=mesh,
        in_specs=(rows, rows, rows, rows, P(), P(), P("groups")),
        out_specs=(rows, rows, rows),
        check_vma=False,
    )
```

```python
import math

import jax
import jax.numpy as jnp
from jax import lax
from jax.experimental import pallas as pl
from jax.experimental.pallas import tpu as pltpu
from jax.sharding import PartitionSpec as P

STEP = 16
WINDOW = 16
ORDER = tuple(range(WINDOW - 1, 0, -1))
FLOOR = -1e30
LOG2E = 1.4426950408889634
EARLY_HEADS = 8
VMEM_LIMIT = 48 * 2**20

BF = jnp.bfloat16
F32 = jnp.float32


def nn(a, b):
    return lax.dot_general(a, b, (((1,), (0,)), ((), ())), preferred_element_type=F32)


def nt(a, b):
    return lax.dot_general(a, b, (((1,), (1,)), ((), ())), preferred_element_type=F32)


def tn(a, b):
    return lax.dot_general(a, b, (((0,), (0,)), ((), ())), preferred_element_type=F32)


def parts_of(x, count):
    out = []
    for _ in range(count - 1):
        head = x.astype(BF).astype(F32)
        out.append(head)
        x = x - head
    out.append(x)
    return out


def rows_block(rows, height, width):
    at = lax.broadcasted_iota(jnp.int32, (height, width), 0)
    block = jnp.zeros((height, width), F32)
    for n, row in enumerate(rows):
        block = jnp.where(at == n, row, block)
    return block


def kernel(
    span_ref, res_ref, count_hbm, q_hbm, k_hbm, v_hbm, g_hbm,
    dq_ref, dk_ref, dv_ref, q_ref, k_ref, v_ref, g_ref, load_sem, qt, kt, vt, gt, dqt, dkt, dvt, qb, gb, pick, far, pb, dpb,
    send1, recv1, send2, recv2, ss1, rs1, ss2, rs2, count_ref, count_sem,
):
    tokens, width = q_ref.shape
    heads = span_ref.shape[0]
    dim = width // heads
    few = tokens // STEP
    chosen = heads * few
    scale = 1.0 / math.sqrt(dim)
    scale2 = scale * LOG2E
    me = lax.axis_index("seq")
    base = (me // WINDOW) * WINDOW
    my = me - base
    count_copy = pltpu.make_async_copy(count_hbm, count_ref, count_sem)
    count_copy.start()
    loads = [
        pltpu.make_async_copy(source, target, load_sem.at[n])
        for n, (source, target) in enumerate(
            ((q_hbm, q_ref), (g_hbm, g_ref), (k_hbm, k_ref), (v_hbm, v_ref))
        )
    ]
    for load in loads:
        load.start()

    bits = [lax.rem(my // b, 2) for b in (1, 2, 4, 8)]

    def partner(n):
        to = my
        for at, b in enumerate((1, 2, 4, 8)):
            if n & b:
                to = to + b - 2 * b * bits[at]
        return to

    barrier = pltpu.get_barrier_semaphore()

    for n in ORDER:
        pl.semaphore_signal(
            barrier, inc=1, device_id={"seq": base + partner(n)},
            device_id_type=pl.DeviceIdType.MESH,
        )

    def block_of(n):
        return pl.ds(pl.multiple_of(n * few, few), few)

    def exchange(n, source, target, send_sem, recv_sem):
        to = partner(n)
        return pltpu.make_async_remote_copy(
            src_ref=source.at[block_of(to)],
            dst_ref=target.at[block_of(my)],
            send_sem=send_sem.at[n],
            recv_sem=recv_sem.at[n],
            device_id={"seq": base + to},
            device_id_type=pl.DeviceIdType.MESH,
        )

    def start_all(*args):
        for n in ORDER:
            exchange(n, *args).start()

    def wait_all(*args):
        for n in ORDER[::-1]:
            exchange(n, *args).wait_recv()

    def wait_sent(*args):
        for n in ORDER:
            exchange(n, *args).wait_send()

    count_copy.wait()
    count = count_ref[0]
    lane = lax.broadcasted_iota(jnp.int32, (1, chosen), 1)
    lane_head = lane // few
    lane_res = jnp.zeros((1, chosen), jnp.int32)
    lane_span = jnp.zeros((1, chosen), jnp.int32)
    for h in range(heads):
        lane_res = jnp.where(lane_head == h, res_ref[h], lane_res)
        lane_span = jnp.where(lane_head == h, span_ref[h], lane_span)
    lane_token = (lane % few) * STEP + lane_res
    row = lax.broadcasted_iota(jnp.int32, (tokens, tokens), 0)
    col = lax.broadcasted_iota(jnp.int32, (tokens, tokens), 1)
    start = me * tokens
    huge = jnp.int32(1 << 20)
    row_ok = row + start < count
    far[...] = jnp.where(row_ok, row ^ col, huge)
    pick[...] = (row == lane_token).astype(F32).astype(BF)

    for load, source, target in zip(
        loads, (q_ref, g_ref, k_ref, v_ref), (qt, gt, kt, vt)
    ):
        load.wait()
        target[...] = source[...].T

    def picked(source, keep):
        full = nn(source[...], pick[...])
        total = jnp.zeros((dim, chosen), F32)
        for h in range(heads):
            part = jnp.where(lane_head == h, full[h * dim : (h + 1) * dim], 0.0)
            if keep is not None:
                keep[h * dim : (h + 1) * dim, :] = part.astype(BF)
            total = total + part
        return total

    q_few = picked(qt, qb)
    g_few = picked(gt, gb)
    k_few = picked(kt, None)
    v_few = picked(vt, None)

    mask = jnp.where(row_ok, row ^ lane_token, huge) < lane_span
    s = jnp.where(mask, nn(k_ref[...], qb[...]) * scale2, FLOOR)
    top = jnp.max(s, axis=0, keepdims=True)
    p = jnp.exp2(s - top)
    total = jnp.sum(p, axis=0, keepdims=True)
    p = p * (1.0 / total)
    dp = nn(v_ref[...], gb[...])
    local_lse = top + jnp.log(total) * LOG2E
    local_delta = jnp.sum(p * dp, axis=0, keepdims=True)
    pb[...] = p
    dpb[...] = dp
    tail = chosen - 4 * dim
    stats = rows_block(parts_of(local_lse, 3) + parts_of(local_delta, 2), tail, chosen)
    packed = jnp.concatenate([q_few, k_few, v_few, g_few, stats], axis=0)
    send1[...] = packed.T.astype(BF)

    pl.semaphore_wait(barrier, WINDOW - 1)
    start_all(send1, recv1, ss1, rs1)
    recv1[block_of(my), :] = send1[block_of(my), :]

    query_ok = lane + start < count

    def local_head(h, carry):
        at = pl.ds(pl.multiple_of(h * dim, 16), dim)
        qh, kh, vh, gh = qt[at, :], kt[at, :], vt[at, :], gt[at, :]
        s = jnp.where(far[...] < span_ref[h], tn(kh, qh) * scale2, FLOOR)
        top = jnp.max(s, axis=0, keepdims=True)
        p = jnp.exp2(s - top)
        inverse = 1.0 / jnp.sum(p, axis=0, keepdims=True)
        dp = tn(vh, gh)
        delta = jnp.sum(p * dp, axis=0, keepdims=True) * inverse
        keep = query_ok & (lane % STEP != res_ref[h])
        w = p * jnp.where(keep, inverse, 0.0)
        ds = (w * (dp - delta)).astype(BF)
        dqt[at, :] = nn(kh, ds) * scale
        dkt[at, :] = nt(qh, ds) * scale
        dvt[at, :] = nt(gh, w.astype(BF))
        return carry

    lax.fori_loop(0, EARLY_HEADS, local_head, 0, unroll=4)

    wait_all(send1, recv1, ss1, rs1)
    got = recv1[...].astype(F32).T
    got_half = got.astype(BF)
    qh, kh = got_half[0:dim], got_half[dim : 2 * dim]
    vh, gh = got_half[2 * dim : 3 * dim], got_half[3 * dim : 4 * dim]
    at = 4 * dim
    local_lse = got[at : at + 1] + got[at + 1 : at + 2] + got[at + 2 : at + 3]
    local_delta = got[at + 3 : at + 4] + got[at + 4 : at + 5]
    limit = count - base * tokens - res_ref[my]
    s = jnp.where(row * STEP < limit, tn(kh, qh) * scale2, FLOOR)
    top = jnp.max(s, axis=0, keepdims=True)
    p = jnp.exp2(s - top)
    total = jnp.sum(p, axis=0, keepdims=True)
    dilated_lse = top + jnp.log(total) * LOG2E
    most = jnp.maximum(local_lse, dilated_lse)
    both = most + jnp.log(jnp.exp2(local_lse - most) + jnp.exp2(dilated_lse - most)) * LOG2E
    here_ok = lane * STEP < limit
    local_part = jnp.where(here_ok, jnp.exp2(local_lse - both), 0.0)
    u = p * jnp.where(here_ok, jnp.exp2(top - both), 0.0)
    dp = tn(vh, gh)
    delta = local_part * local_delta + jnp.sum(u * dp, axis=0, keepdims=True)
    delta = jnp.where(here_ok, delta, 0.0)
    ds = (u * (dp - delta)).astype(BF)
    stats = rows_block(parts_of(local_part, 2) + parts_of(delta, 2), chosen - 3 * dim, chosen)
    packed = jnp.concatenate(
        [nn(kh, ds) * scale, nt(qh, ds) * scale, nt(gh, u.astype(BF)), stats], axis=0
    )
    send2[...] = packed.T.astype(BF)
    start_all(send2, recv2, ss2, rs2)
    recv2[block_of(my), :] = send2[block_of(my), :]

    lax.fori_loop(EARLY_HEADS, heads, local_head, 0, unroll=4)

    wait_all(send2, recv2, ss2, rs2)
    back = recv2[...].astype(F32).T
    at = 3 * dim
    local_part = back[at : at + 1] + back[at + 1 : at + 2]
    delta = back[at + 2 : at + 3] + back[at + 3 : at + 4]
    w = pb[...] * local_part
    ds = (w * (dpb[...] - delta)).astype(BF)
    wide = nn(kt[...], ds) * scale
    dq_few, dk_few, dv_few = back[0:dim], back[dim : 2 * dim], back[2 * dim : 3 * dim]

    def spread(piece_of):
        pieces = [
            jnp.where(lane_head == h, piece_of(h), 0.0).astype(BF) for h in range(heads)
        ]
        return nt(jnp.concatenate(pieces, axis=0), pick[...])

    dq = dqt[...] + spread(lambda h: wide[h * dim : (h + 1) * dim] + dq_few)
    dq_ref[...] = dq.astype(BF)
    dk = dkt[...] + nt(qb[...], ds) * scale + spread(lambda h: dk_few)
    dk_ref[...] = dk.astype(BF)
    dv = dvt[...] + nt(gb[...], w.astype(BF)) + spread(lambda h: dv_few)
    dv_ref[...] = dv.astype(BF)
    wait_sent(send1, recv1, ss1, rs1)
    wait_sent(send2, recv2, ss2, rs2)


def finish(a_in, b_in, c_in, a_out, b_out, c_out, targets, store_sem):
    stores = []
    for n, (source, target) in enumerate(((a_in, a_out), (b_in, b_out), (c_in, c_out))):
        targets[n] = source[...].T
        store = pltpu.make_async_copy(targets.at[n], target, store_sem.at[n])
        store.start()
        stores.append(store)
    for store in stores:
        store.wait()


def shards(queries, keys, values, grad_out, local_span, head_residue, valid_count):
    tokens, width = queries.shape
    heads = local_span.shape[0]
    chosen = heads * (tokens // STEP)
    assert heads == WINDOW and chosen == tokens
    smem = pl.BlockSpec(memory_space=pltpu.SMEM)
    vmem = pl.BlockSpec(memory_space=pltpu.VMEM)
    hbm = pl.BlockSpec(memory_space=pltpu.MemorySpace.HBM)
    out = jax.ShapeDtypeStruct((tokens, width), BF)
    turned = pltpu.VMEM((width, tokens), BF)
    gradients = pl.pallas_call(
        kernel,
        out_shape=(turned, turned, turned),
        in_specs=[smem] * 2 + [hbm] * 5,
        out_specs=(vmem, vmem, vmem),
        scratch_shapes=[pltpu.VMEM((tokens, width), BF)] * 4
        + [pltpu.SemaphoreType.DMA((4,))]
        + [pltpu.VMEM((width, tokens), BF)] * 4
        + [pltpu.VMEM((width, tokens), F32)] * 3
        + [pltpu.VMEM((width, chosen), BF)] * 2
        + [
            pltpu.VMEM((tokens, chosen), BF),
            pltpu.VMEM((tokens, tokens), jnp.int32),
            pltpu.VMEM((tokens, chosen), F32),
            pltpu.VMEM((tokens, chosen), F32),
        ]
        + [pltpu.VMEM((chosen, chosen), BF)] * 4
        + [pltpu.SemaphoreType.DMA((WINDOW,))] * 4
        + [pltpu.SMEM((1,), jnp.int32), pltpu.SemaphoreType.DMA],
        compiler_params=pltpu.CompilerParams(
            collective_id=0, has_side_effects=True, vmem_limit_bytes=VMEM_LIMIT
        ),
    )(local_span, head_residue, valid_count, *[
        pltpu.with_memory_space_constraint(x, pltpu.MemorySpace.HBM)
        for x in (queries, keys, values, grad_out)
    ])
    return pl.pallas_call(
        finish,
        out_shape=(out, out, out),
        in_specs=[vmem] * 3,
        out_specs=(hbm, hbm, hbm),
        scratch_shapes=[
            pltpu.VMEM((3, tokens, width), BF),
            pltpu.SemaphoreType.DMA((3,)),
        ],
        compiler_params=pltpu.CompilerParams(vmem_limit_bytes=VMEM_LIMIT),
    )(*[pltpu.with_memory_space_constraint(x, pltpu.MemorySpace.VMEM) for x in gradients])


def solution(mesh):
    rows = P(("groups", "seq"), None)
    return jax.shard_map(
        shards,
        mesh=mesh,
        in_specs=(rows, rows, rows, rows, P(), P(), P("groups")),
        out_specs=(rows, rows, rows),
        check_vma=False,
    )
```

```python
import math

import jax
import jax.numpy as jnp
from jax import lax
from jax.experimental import pallas as pl
from jax.experimental.pallas import tpu as pltpu
from jax.sharding import PartitionSpec as P

STEP = 16
WINDOW = 16
ORDER = tuple(range(WINDOW - 1, 0, -1))
FIRST = (14, 15, 12, 13, 10, 11, 8, 9, 0, 1, 2, 3, 4, 5, 6, 7)
SECOND = (0, 1, 14, 15, 12, 13, 10, 11, 8, 9, 2, 3, 4, 5, 6, 7)
FLOOR = -1e30
LOG2E = 1.4426950408889634
EARLY_HEADS = 8
VMEM_LIMIT = 48 * 2**20

BF = jnp.bfloat16
F32 = jnp.float32


def nn(a, b):
    return lax.dot_general(a, b, (((1,), (0,)), ((), ())), preferred_element_type=F32)


def nt(a, b):
    return lax.dot_general(a, b, (((1,), (1,)), ((), ())), preferred_element_type=F32)


def tn(a, b):
    return lax.dot_general(a, b, (((0,), (0,)), ((), ())), preferred_element_type=F32)


def parts_of(x, count):
    out = []
    for _ in range(count - 1):
        head = x.astype(BF).astype(F32)
        out.append(head)
        x = x - head
    out.append(x)
    return out


def rows_block(rows, height, width):
    at = lax.broadcasted_iota(jnp.int32, (height, width), 0)
    block = jnp.zeros((height, width), F32)
    for n, row in enumerate(rows):
        block = jnp.where(at == n, row, block)
    return block


def kernel(
    span_ref, res_ref, count_hbm, q_hbm, k_hbm, v_hbm, g_hbm,
    dq_ref, dk_ref, dv_ref, q_ref, k_ref, v_ref, g_ref, load_sem, qt, kt, vt, gt, dqt, dkt, dvt, qb, gb, pick, far, pb, dpb,
    send1, recv1, send2, recv2, ss1, rs1, ss2, rs2, count_ref, count_sem,
):
    tokens, width = q_ref.shape
    heads = span_ref.shape[0]
    dim = width // heads
    few = tokens // STEP
    chosen = heads * few
    scale = 1.0 / math.sqrt(dim)
    scale2 = scale * LOG2E
    me = lax.axis_index("seq")
    base = (me // WINDOW) * WINDOW
    my = me - base
    count_copy = pltpu.make_async_copy(count_hbm, count_ref, count_sem)
    count_copy.start()
    loads = [
        pltpu.make_async_copy(source, target, load_sem.at[n])
        for n, (source, target) in enumerate(
            ((q_hbm, q_ref), (g_hbm, g_ref), (k_hbm, k_ref), (v_hbm, v_ref))
        )
    ]
    for load in loads:
        load.start()

    bits = [lax.rem(my // b, 2) for b in (1, 2, 4, 8)]

    def partner(n):
        to = my
        for at, b in enumerate((1, 2, 4, 8)):
            if n & b:
                to = to + b - 2 * b * bits[at]
        return to

    barrier = pltpu.get_barrier_semaphore()

    for n in ORDER:
        pl.semaphore_signal(
            barrier, inc=1, device_id={"seq": base + partner(n)},
            device_id_type=pl.DeviceIdType.MESH,
        )

    def block_of(n):
        return pl.ds(pl.multiple_of(n * few, few), few)

    def exchange(n, source, target, send_sem, recv_sem):
        to = partner(n)
        return pltpu.make_async_remote_copy(
            src_ref=source.at[block_of(to)],
            dst_ref=target.at[block_of(my)],
            send_sem=send_sem.at[to],
            recv_sem=recv_sem.at[to],
            device_id={"seq": base + to},
            device_id_type=pl.DeviceIdType.MESH,
        )

    def send_to(to, source, target, send_sem, recv_sem):
        return pltpu.make_async_remote_copy(
            src_ref=source.at[pl.ds(to * few, few)],
            dst_ref=target.at[block_of(my)],
            send_sem=send_sem.at[to],
            recv_sem=recv_sem.at[my],
            device_id={"seq": base + to},
            device_id_type=pl.DeviceIdType.MESH,
        )

    def start_all(order, *args):
        for to in order:
            @pl.when(my != to)
            def _():
                send_to(to, *args).start()

    def wait_all(*args):
        for n in ORDER[::-1]:
            exchange(n, *args).wait_recv()

    def wait_sent(*args):
        for n in ORDER:
            exchange(n, *args).wait_send()

    count_copy.wait()
    count = count_ref[0]
    lane = lax.broadcasted_iota(jnp.int32, (1, chosen), 1)
    lane_head = lane // few
    lane_res = jnp.zeros((1, chosen), jnp.int32)
    lane_span = jnp.zeros((1, chosen), jnp.int32)
    for h in range(heads):
        lane_res = jnp.where(lane_head == h, res_ref[h], lane_res)
        lane_span = jnp.where(lane_head == h, span_ref[h], lane_span)
    lane_token = (lane % few) * STEP + lane_res
    row = lax.broadcasted_iota(jnp.int32, (tokens, tokens), 0)
    col = lax.broadcasted_iota(jnp.int32, (tokens, tokens), 1)
    start = me * tokens
    huge = jnp.int32(1 << 20)
    row_ok = row + start < count
    far[...] = jnp.where(row_ok, row ^ col, huge)
    pick[...] = (row == lane_token).astype(F32).astype(BF)

    for load, source, target in zip(
        loads, (q_ref, g_ref, k_ref, v_ref), (qt, gt, kt, vt)
    ):
        load.wait()
        target[...] = source[...].T

    def picked(source, keep):
        full = nn(source[...], pick[...])
        total = jnp.zeros((dim, chosen), F32)
        for h in range(heads):
            part = jnp.where(lane_head == h, full[h * dim : (h + 1) * dim], 0.0)
            if keep is not None:
                keep[h * dim : (h + 1) * dim, :] = part.astype(BF)
            total = total + part
        return total

    q_few = picked(qt, qb)
    g_few = picked(gt, gb)
    k_few = picked(kt, None)
    v_few = picked(vt, None)

    mask = jnp.where(row_ok, row ^ lane_token, huge) < lane_span
    s = jnp.where(mask, nn(k_ref[...], qb[...]) * scale2, FLOOR)
    top = jnp.max(s, axis=0, keepdims=True)
    p = jnp.exp2(s - top)
    total = jnp.sum(p, axis=0, keepdims=True)
    p = p * (1.0 / total)
    dp = nn(v_ref[...], gb[...])
    local_lse = top + jnp.log(total) * LOG2E
    local_delta = jnp.sum(p * dp, axis=0, keepdims=True)
    pb[...] = p
    dpb[...] = dp
    tail = chosen - 4 * dim
    stats = rows_block(parts_of(local_lse, 3) + parts_of(local_delta, 2), tail, chosen)
    packed = jnp.concatenate([q_few, k_few, v_few, g_few, stats], axis=0)
    send1[...] = packed.T.astype(BF)

    pl.semaphore_wait(barrier, WINDOW - 1)
    start_all(FIRST, send1, recv1, ss1, rs1)
    recv1[block_of(my), :] = send1[block_of(my), :]

    query_ok = lane + start < count

    def local_head(h, carry):
        at = pl.ds(pl.multiple_of(h * dim, 16), dim)
        qh, kh, vh, gh = qt[at, :], kt[at, :], vt[at, :], gt[at, :]
        s = jnp.where(far[...] < span_ref[h], tn(kh, qh) * scale2, FLOOR)
        top = jnp.max(s, axis=0, keepdims=True)
        p = jnp.exp2(s - top)
        inverse = 1.0 / jnp.sum(p, axis=0, keepdims=True)
        dp = tn(vh, gh)
        delta = jnp.sum(p * dp, axis=0, keepdims=True) * inverse
        keep = query_ok & (lane % STEP != res_ref[h])
        w = p * jnp.where(keep, inverse, 0.0)
        ds = (w * (dp - delta)).astype(BF)
        dqt[at, :] = nn(kh, ds) * scale
        dkt[at, :] = nt(qh, ds) * scale
        dvt[at, :] = nt(gh, w.astype(BF))
        return carry

    lax.fori_loop(0, EARLY_HEADS, local_head, 0, unroll=4)

    wait_all(send1, recv1, ss1, rs1)
    got = recv1[...].astype(F32).T
    got_half = got.astype(BF)
    qh, kh = got_half[0:dim], got_half[dim : 2 * dim]
    vh, gh = got_half[2 * dim : 3 * dim], got_half[3 * dim : 4 * dim]
    at = 4 * dim
    local_lse = got[at : at + 1] + got[at + 1 : at + 2] + got[at + 2 : at + 3]
    local_delta = got[at + 3 : at + 4] + got[at + 4 : at + 5]
    limit = count - base * tokens - res_ref[my]
    s = jnp.where(row * STEP < limit, tn(kh, qh) * scale2, FLOOR)
    top = jnp.max(s, axis=0, keepdims=True)
    p = jnp.exp2(s - top)
    total = jnp.sum(p, axis=0, keepdims=True)
    dilated_lse = top + jnp.log(total) * LOG2E
    most = jnp.maximum(local_lse, dilated_lse)
    both = most + jnp.log(jnp.exp2(local_lse - most) + jnp.exp2(dilated_lse - most)) * LOG2E
    here_ok = lane * STEP < limit
    local_part = jnp.where(here_ok, jnp.exp2(local_lse - both), 0.0)
    u = p * jnp.where(here_ok, jnp.exp2(top - both), 0.0)
    dp = tn(vh, gh)
    delta = local_part * local_delta + jnp.sum(u * dp, axis=0, keepdims=True)
    delta = jnp.where(here_ok, delta, 0.0)
    ds = (u * (dp - delta)).astype(BF)
    stats = rows_block(parts_of(local_part, 2) + parts_of(delta, 2), chosen - 3 * dim, chosen)
    packed = jnp.concatenate(
        [nn(kh, ds) * scale, nt(qh, ds) * scale, nt(gh, u.astype(BF)), stats], axis=0
    )
    send2[...] = packed.T.astype(BF)
    start_all(SECOND, send2, recv2, ss2, rs2)
    recv2[block_of(my), :] = send2[block_of(my), :]

    lax.fori_loop(EARLY_HEADS, heads, local_head, 0, unroll=4)

    wait_all(send2, recv2, ss2, rs2)
    back = recv2[...].astype(F32).T
    at = 3 * dim
    local_part = back[at : at + 1] + back[at + 1 : at + 2]
    delta = back[at + 2 : at + 3] + back[at + 3 : at + 4]
    w = pb[...] * local_part
    ds = (w * (dpb[...] - delta)).astype(BF)
    wide = nn(kt[...], ds) * scale
    dq_few, dk_few, dv_few = back[0:dim], back[dim : 2 * dim], back[2 * dim : 3 * dim]

    def spread(piece_of):
        pieces = [
            jnp.where(lane_head == h, piece_of(h), 0.0).astype(BF) for h in range(heads)
        ]
        return nt(jnp.concatenate(pieces, axis=0), pick[...])

    dq = dqt[...] + spread(lambda h: wide[h * dim : (h + 1) * dim] + dq_few)
    dq_ref[...] = dq.astype(BF)
    dk = dkt[...] + nt(qb[...], ds) * scale + spread(lambda h: dk_few)
    dk_ref[...] = dk.astype(BF)
    dv = dvt[...] + nt(gb[...], w.astype(BF)) + spread(lambda h: dv_few)
    dv_ref[...] = dv.astype(BF)
    wait_sent(send1, recv1, ss1, rs1)
    wait_sent(send2, recv2, ss2, rs2)


def finish(a_in, b_in, c_in, a_out, b_out, c_out, targets, store_sem):
    stores = []
    for n, (source, target) in enumerate(((a_in, a_out), (b_in, b_out), (c_in, c_out))):
        targets[n] = source[...].T
        store = pltpu.make_async_copy(targets.at[n], target, store_sem.at[n])
        store.start()
        stores.append(store)
    for store in stores:
        store.wait()


def shards(queries, keys, values, grad_out, local_span, head_residue, valid_count):
    tokens, width = queries.shape
    heads = local_span.shape[0]
    chosen = heads * (tokens // STEP)
    assert heads == WINDOW and chosen == tokens
    smem = pl.BlockSpec(memory_space=pltpu.SMEM)
    vmem = pl.BlockSpec(memory_space=pltpu.VMEM)
    hbm = pl.BlockSpec(memory_space=pltpu.MemorySpace.HBM)
    out = jax.ShapeDtypeStruct((tokens, width), BF)
    turned = pltpu.VMEM((width, tokens), BF)
    gradients = pl.pallas_call(
        kernel,
        out_shape=(turned, turned, turned),
        in_specs=[smem] * 2 + [hbm] * 5,
        out_specs=(vmem, vmem, vmem),
        scratch_shapes=[pltpu.VMEM((tokens, width), BF)] * 4
        + [pltpu.SemaphoreType.DMA((4,))]
        + [pltpu.VMEM((width, tokens), BF)] * 4
        + [pltpu.VMEM((width, tokens), F32)] * 3
        + [pltpu.VMEM((width, chosen), BF)] * 2
        + [
            pltpu.VMEM((tokens, chosen), BF),
            pltpu.VMEM((tokens, tokens), jnp.int32),
            pltpu.VMEM((tokens, chosen), F32),
            pltpu.VMEM((tokens, chosen), F32),
        ]
        + [pltpu.VMEM((chosen, chosen), BF)] * 4
        + [pltpu.SemaphoreType.DMA((WINDOW,))] * 4
        + [pltpu.SMEM((1,), jnp.int32), pltpu.SemaphoreType.DMA],
        compiler_params=pltpu.CompilerParams(
            collective_id=0, has_side_effects=True, vmem_limit_bytes=VMEM_LIMIT
        ),
    )(local_span, head_residue, valid_count, *[
        pltpu.with_memory_space_constraint(x, pltpu.MemorySpace.HBM)
        for x in (queries, keys, values, grad_out)
    ])
    return pl.pallas_call(
        finish,
        out_shape=(out, out, out),
        in_specs=[vmem] * 3,
        out_specs=(hbm, hbm, hbm),
        scratch_shapes=[
            pltpu.VMEM((3, tokens, width), BF),
            pltpu.SemaphoreType.DMA((3,)),
        ],
        compiler_params=pltpu.CompilerParams(vmem_limit_bytes=VMEM_LIMIT),
    )(*[pltpu.with_memory_space_constraint(x, pltpu.MemorySpace.VMEM) for x in gradients])


def solution(mesh):
    rows = P(("groups", "seq"), None)
    return jax.shard_map(
        shards,
        mesh=mesh,
        in_specs=(rows, rows, rows, rows, P(), P(), P("groups")),
        out_specs=(rows, rows, rows),
        check_vma=False,
    )
```

```python
import math

import jax
import jax.numpy as jnp
from jax import lax
from jax.experimental import pallas as pl
from jax.experimental.pallas import tpu as pltpu
from jax.sharding import PartitionSpec as P

STEP = 16
WINDOW = 16
ORDER = tuple(range(WINDOW - 1, 0, -1))
FIRST = (14, 15, 12, 13, 10, 11, 8, 9, 0, 1, 2, 3, 4, 5, 6, 7)
SECOND = (0, 1, 14, 15, 12, 13, 10, 11, 8, 9, 2, 3, 4, 5, 6, 7)
HALF = 128
FLOOR = -1e30
LOG2E = 1.4426950408889634
EARLY_HEADS = 8
VMEM_LIMIT = 48 * 2**20

BF = jnp.bfloat16
F32 = jnp.float32


def nn(a, b):
    return lax.dot_general(a, b, (((1,), (0,)), ((), ())), preferred_element_type=F32)


def nt(a, b):
    return lax.dot_general(a, b, (((1,), (1,)), ((), ())), preferred_element_type=F32)


def tn(a, b):
    return lax.dot_general(a, b, (((0,), (0,)), ((), ())), preferred_element_type=F32)


def parts_of(x, count):
    out = []
    for _ in range(count - 1):
        head = x.astype(BF).astype(F32)
        out.append(head)
        x = x - head
    out.append(x)
    return out


def rows_block(rows, height, width):
    at = lax.broadcasted_iota(jnp.int32, (height, width), 0)
    block = jnp.zeros((height, width), F32)
    for n, row in enumerate(rows):
        block = jnp.where(at == n, row, block)
    return block


def gather_rows(at, *counts):
    row = lax.broadcasted_iota(jnp.int32, (16, HALF), 0)
    lane = lax.broadcasted_iota(jnp.int32, (16, HALF), 1)
    total = jnp.zeros((16, HALF), F32)
    for n, count in enumerate(counts):
        hit = (row == n) & (lane >= at) & (lane < at + count)
        total = jnp.where(hit, 1.0, total)
        at += count
    return total.astype(BF)


def kernel(
    span_ref, res_ref, count_hbm, q_hbm, k_hbm, v_hbm, g_hbm,
    dq_ref, dk_ref, dv_ref, back_ref, pb, dpb, qb, gb, k_ref, here_ref,
    q_ref, v_ref, g_ref, load_sem, qt, kt, vt, gt, dqt, dkt, dvt, pick, far, w_ref, ds_ref,
    send1, recv1, send2, recv2, ss1, rs1, ss2, rs2, count_ref, count_sem,
):
    tokens, width = q_ref.shape
    heads = span_ref.shape[0]
    dim = width // heads
    few = tokens // STEP
    chosen = heads * few
    scale = 1.0 / math.sqrt(dim)
    scale2 = scale * LOG2E
    me = lax.axis_index("seq")
    base = (me // WINDOW) * WINDOW
    my = me - base
    count_copy = pltpu.make_async_copy(count_hbm, count_ref, count_sem)
    count_copy.start()
    loads = [
        pltpu.make_async_copy(source, target, load_sem.at[n])
        for n, (source, target) in enumerate(
            ((q_hbm, q_ref), (g_hbm, g_ref), (k_hbm, k_ref), (v_hbm, v_ref))
        )
    ]
    for load in loads:
        load.start()

    bits = [lax.rem(my // b, 2) for b in (1, 2, 4, 8)]

    def partner(n):
        to = my
        for at, b in enumerate((1, 2, 4, 8)):
            if n & b:
                to = to + b - 2 * b * bits[at]
        return to

    barrier = pltpu.get_barrier_semaphore()

    for n in ORDER:
        pl.semaphore_signal(
            barrier, inc=1, device_id={"seq": base + partner(n)},
            device_id_type=pl.DeviceIdType.MESH,
        )

    def block_of(n):
        return pl.ds(pl.multiple_of(n * few, few), few)

    def send_to(to, source, target, send_sem, recv_sem):
        return pltpu.make_async_remote_copy(
            src_ref=source.at[pl.ds(to * few, few)],
            dst_ref=target.at[block_of(my)],
            send_sem=send_sem,
            recv_sem=recv_sem,
            device_id={"seq": base + to},
            device_id_type=pl.DeviceIdType.MESH,
        )

    def start_all(order, *args):
        for to in order:
            @pl.when(my != to)
            def _():
                send_to(to, *args).start()

    def all_of(source, target, send_sem, recv_sem):
        others = pl.ds(0, (WINDOW - 1) * few)
        return pltpu.make_async_remote_copy(
            src_ref=source.at[others],
            dst_ref=target.at[others],
            send_sem=send_sem,
            recv_sem=recv_sem,
            device_id={"seq": base + partner(1)},
            device_id_type=pl.DeviceIdType.MESH,
        )

    def wait_all(*args):
        all_of(*args).wait_recv()

    def wait_sent(*args):
        all_of(*args).wait_send()

    count_copy.wait()
    count = count_ref[0]
    lane = lax.broadcasted_iota(jnp.int32, (1, chosen), 1)
    lane_head = lane // few
    lane_res = jnp.zeros((1, chosen), jnp.int32)
    lane_span = jnp.zeros((1, chosen), jnp.int32)
    for h in range(heads):
        lane_res = jnp.where(lane_head == h, res_ref[h], lane_res)
        lane_span = jnp.where(lane_head == h, span_ref[h], lane_span)
    lane_token = (lane % few) * STEP + lane_res
    row = lax.broadcasted_iota(jnp.int32, (tokens, tokens), 0)
    col = lax.broadcasted_iota(jnp.int32, (tokens, tokens), 1)
    start = me * tokens
    huge = jnp.int32(1 << 20)
    row_ok = row + start < count
    far[...] = jnp.where(row_ok, row ^ col, huge)
    pick[...] = (row == lane_token).astype(F32).astype(BF)

    for load, source, target in zip(
        loads, (q_ref, g_ref, k_ref, v_ref), (qt, gt, kt, vt)
    ):
        load.wait()
        target[...] = source[...].T

    def picked(source, keep):
        full = nn(source[...], pick[...])
        total = jnp.zeros((dim, chosen), F32)
        for h in range(heads):
            part = jnp.where(lane_head == h, full[h * dim : (h + 1) * dim], 0.0)
            if keep is not None:
                keep[h * dim : (h + 1) * dim, :] = part.astype(BF)
            total = total + part
        return total

    q_few = picked(qt, qb)
    g_few = picked(gt, gb)
    k_few = picked(kt, None)
    v_few = picked(vt, None)

    mask = jnp.where(row_ok, row ^ lane_token, huge) < lane_span
    s = jnp.where(mask, nn(k_ref[...], qb[...]) * scale2, FLOOR)
    top = jnp.max(s, axis=0, keepdims=True)
    p = jnp.exp2(s - top)
    total = jnp.sum(p, axis=0, keepdims=True)
    p = p * (1.0 / total)
    dp = nn(v_ref[...], gb[...])
    local_lse = top + jnp.log(total) * LOG2E
    local_delta = jnp.sum(p * dp, axis=0, keepdims=True)
    pb[...] = p
    dpb[...] = dp
    gap = HALF // 2 - dim
    stats = rows_block(parts_of(local_lse, 3) + parts_of(local_delta, 2), gap, chosen)
    blank = jnp.zeros((gap, chosen), F32)
    packed = jnp.concatenate(
        [q_few, stats, v_few, blank, k_few, blank, g_few, blank], axis=0
    )
    send1[...] = packed.T.astype(BF)

    pl.semaphore_wait(barrier, WINDOW - 1)
    start_all(FIRST, send1, recv1, ss1, rs1)
    recv1[block_of(my), :] = send1[block_of(my), :]

    query_ok = lane + start < count

    def head_at(h):
        return pl.ds(pl.multiple_of(h * dim, 16), dim)

    def weigh(h, slot):
        at = head_at(h)
        qh, kh, vh, gh = qt[at, :], kt[at, :], vt[at, :], gt[at, :]
        s = jnp.where(far[...] < span_ref[h], tn(kh, qh) * scale2, FLOOR)
        top = jnp.max(s, axis=0, keepdims=True)
        p = jnp.exp2(s - top)
        inverse = 1.0 / jnp.sum(p, axis=0, keepdims=True)
        dp = tn(vh, gh)
        delta = jnp.sum(p * dp, axis=0, keepdims=True) * inverse
        keep = query_ok & (lane % STEP != res_ref[h])
        w = p * jnp.where(keep, inverse, 0.0)
        w_ref[slot] = w.astype(BF)
        ds_ref[slot] = (w * (dp - delta)).astype(BF)

    def gather(h, slot):
        at = head_at(h)
        dqt[at, :] = nn(kt[at, :], ds_ref[slot]) * scale
        dkt[at, :] = nt(qt[at, :], ds_ref[slot]) * scale
        dvt[at, :] = nt(gt[at, :], w_ref[slot])

    def local_heads(first, last):
        weigh(first, 0)
        weigh(first + 1, 1)

        def pair(n, carry):
            h = first + 2 * n
            gather(h - 2, 0)
            weigh(h, 0)
            gather(h - 1, 1)
            weigh(h + 1, 1)
            return carry

        lax.fori_loop(1, (last - first) // 2, pair, 0)
        gather(last - 2, 0)
        gather(last - 1, 1)

    local_heads(0, EARLY_HEADS)

    wait_all(send1, recv1, ss1, rs1)
    at = lax.broadcasted_iota(jnp.int32, (1, HALF), 1)
    low = at < HALF // 2
    first = jnp.where(at < dim, 1.0, 0.0).astype(BF)
    second = jnp.where((at >= HALF // 2) & (at < HALF // 2 + dim), 1.0, 0.0).astype(BF)
    left, right = recv1[:, :HALF], recv1[:, HALF:]
    limit = count - base * tokens - res_ref[my]
    s = jnp.where(row * STEP < limit, nt(right * first, left) * scale2, FLOOR)
    stats = nt(gather_rows(dim, 3, 2), left)
    local_lse, local_delta = stats[0:1], stats[1:2]
    dp = nt(left * second, right)
    top = jnp.max(s, axis=0, keepdims=True)
    p = jnp.exp2(s - top)
    total = jnp.sum(p, axis=0, keepdims=True)
    dilated_lse = top + jnp.log(total) * LOG2E
    most = jnp.maximum(local_lse, dilated_lse)
    both = most + jnp.log(jnp.exp2(local_lse - most) + jnp.exp2(dilated_lse - most)) * LOG2E
    here_ok = lane * STEP < limit
    local_part = jnp.where(here_ok, jnp.exp2(local_lse - both), 0.0)
    u = p * jnp.where(here_ok, jnp.exp2(top - both), 0.0)
    delta = local_part * local_delta + jnp.sum(u * dp, axis=0, keepdims=True)
    delta = jnp.where(here_ok, delta, 0.0)
    ds = (u * (dp - delta)).astype(BF)
    stats = rows_block(parts_of(local_part, 2) + parts_of(delta, 2), 16, chosen)
    dk_dv = jnp.where(low, nn(ds, left) * scale, nn(u.astype(BF), right))
    send2[:, :HALF] = dk_dv.astype(BF)
    place = lax.broadcasted_iota(jnp.int32, (16, HALF), 0) + HALF // 2
    place = (place == lax.broadcasted_iota(jnp.int32, (16, HALF), 1)).astype(F32)
    dq_stats = jnp.where(low, tn(ds, right) * scale, tn(stats.astype(BF), place.astype(BF)))
    send2[:, HALF:] = dq_stats.astype(BF)
    start_all(SECOND, send2, recv2, ss2, rs2)
    recv2[block_of(my), :] = send2[block_of(my), :]

    local_heads(EARLY_HEADS, heads)

    dq_ref[...] = dqt[...].T
    dk_ref[...] = dkt[...].T
    dv_ref[...] = dvt[...].T
    wide = lax.broadcasted_iota(jnp.int32, (STEP, width), 1)
    wide_res = jnp.zeros((STEP, width), jnp.int32)
    for h in range(heads):
        wide_res = jnp.where(wide >= h * dim, res_ref[h], wide_res)
    at = lax.broadcasted_iota(jnp.int32, (STEP, width), 0)
    here_ref[...] = (at == wide_res).astype(F32)

    wait_all(send2, recv2, ss2, rs2)
    back_ref[...] = recv2[...]
    wait_sent(send1, recv1, ss1, rs1)
    wait_sent(send2, recv2, ss2, rs2)


def finish(
    dq_in, dk_in, dv_in, back, pb, dpb, qb, gb, k_ref, here,
    dq_hbm, dk_hbm, dv_hbm, staged, few, ds_ref, w_ref, store_sem,
):
    tokens, width = dq_in.shape
    chosen = pb.shape[1]
    heads = chosen // STEP
    dim = width // heads
    scale = 1.0 / math.sqrt(dim)
    half, lanes = chosen // 2, width // 2
    stats = nt(gather_rows(HALF // 2, 2, 2), back[:, HALF:])
    w = pb[...] * stats[0:1]
    w_ref[...] = w.astype(BF)
    ds_ref[...] = (w * ((dpb[...] - stats[1:2]) * scale)).astype(BF)
    at = lax.broadcasted_iota(jnp.int32, (STEP, HALF), 1)

    def tiles_of(h):
        first = h * dim // HALF
        return range(first, (h * dim + dim - 1) // HALF + 1)

    def gathered(piece_of):
        tiles = [jnp.zeros((STEP, HALF), F32) for _ in range(width // HALF)]
        for h in range(heads):
            for n in tiles_of(h):
                start = h * dim - n * HALF
                here_too = (at >= start) & (at < start + dim)
                tiles[n] = jnp.where(here_too, piece_of(h, n), tiles[n])
        return jnp.concatenate(tiles, axis=1)

    def sent(column, start):
        def piece(h, n):
            block = back[h * STEP : (h + 1) * STEP, column * HALF : (column + 1) * HALF]
            return pltpu.roll(block.astype(F32), (h * dim - start) % HALF, axis=1)

        return piece

    def emit(n, source, product, target):
        for t in range(tokens // STEP):
            rows = slice(t * STEP, (t + 1) * STEP)
            value = source[rows] + here[...] * few[n, t : t + 1, :]
            if product is not None:
                value = value + product[rows]
            staged[n, rows] = value.astype(BF)
        copy = pltpu.make_async_copy(staged.at[n], target, store_sem.at[n])
        copy.start()
        return copy

    few[0] = gathered(sent(0, HALF // 2))
    few[1] = gathered(sent(0, 0))
    store_dv = emit(0, dv_in, nt(w_ref[...], gb[...]), dv_hbm)
    store_dk = emit(1, dk_in, nt(ds_ref[...], qb[...]), dk_hbm)
    own = [
        tn(ds_ref[:, n * half : (n + 1) * half], k_ref[:, n * lanes : (n + 1) * lanes])
        for n in range(2)
    ]

    def own_piece(h, n):
        side = h * STEP // half
        block = own[side][h * STEP - side * half : (h + 1) * STEP - side * half]
        block = block[:, n * HALF - side * lanes : (n + 1) * HALF - side * lanes]
        return block + sent(1, 0)(h, n)

    few[2] = gathered(own_piece)
    store_dq = emit(2, dq_in, None, dq_hbm)
    store_dv.wait()
    store_dk.wait()
    store_dq.wait()


def shards(queries, keys, values, grad_out, local_span, head_residue, valid_count):
    tokens, width = queries.shape
    heads = local_span.shape[0]
    chosen = heads * (tokens // STEP)
    assert heads == WINDOW and chosen == tokens
    smem = pl.BlockSpec(memory_space=pltpu.SMEM)
    vmem = pl.BlockSpec(memory_space=pltpu.VMEM)
    hbm = pl.BlockSpec(memory_space=pltpu.MemorySpace.HBM)
    out = jax.ShapeDtypeStruct((tokens, width), BF)
    full = pltpu.VMEM((tokens, width), F32)
    passed = pl.pallas_call(
        kernel,
        out_shape=(full, full, full)
        + (
            pltpu.VMEM((chosen, chosen), BF),
            pltpu.VMEM((tokens, chosen), F32),
            pltpu.VMEM((tokens, chosen), F32),
            pltpu.VMEM((width, chosen), BF),
            pltpu.VMEM((width, chosen), BF),
            pltpu.VMEM((tokens, width), BF),
            pltpu.VMEM((STEP, width), F32),
        ),
        in_specs=[smem] * 2 + [hbm] * 5,
        out_specs=(vmem,) * 10,
        scratch_shapes=[pltpu.VMEM((tokens, width), BF)] * 3
        + [pltpu.SemaphoreType.DMA((4,))]
        + [pltpu.VMEM((width, tokens), BF)] * 4
        + [pltpu.VMEM((width, tokens), F32)] * 3
        + [
            pltpu.VMEM((tokens, chosen), BF),
            pltpu.VMEM((tokens, tokens), jnp.int32),
            pltpu.VMEM((2, tokens, tokens), BF),
            pltpu.VMEM((2, tokens, tokens), BF),
        ]
        + [pltpu.VMEM((chosen, chosen), BF)] * 4
        + [pltpu.SemaphoreType.DMA] * 4
        + [pltpu.SMEM((1,), jnp.int32), pltpu.SemaphoreType.DMA],
        compiler_params=pltpu.CompilerParams(
            collective_id=0, has_side_effects=True, vmem_limit_bytes=VMEM_LIMIT
        ),
    )(local_span, head_residue, valid_count, *[
        pltpu.with_memory_space_constraint(x, pltpu.MemorySpace.HBM)
        for x in (queries, keys, values, grad_out)
    ])
    return pl.pallas_call(
        finish,
        out_shape=(out, out, out),
        in_specs=[vmem] * 10,
        out_specs=(hbm, hbm, hbm),
        scratch_shapes=[
            pltpu.VMEM((3, tokens, width), BF),
            pltpu.VMEM((3, STEP, width), F32),
            pltpu.VMEM((tokens, chosen), BF),
            pltpu.VMEM((tokens, chosen), BF),
            pltpu.SemaphoreType.DMA((3,)),
        ],
        compiler_params=pltpu.CompilerParams(vmem_limit_bytes=VMEM_LIMIT),
    )(*[pltpu.with_memory_space_constraint(x, pltpu.MemorySpace.VMEM) for x in passed])


def solution(mesh):
    rows = P(("groups", "seq"), None)
    return jax.shard_map(
        shards,
        mesh=mesh,
        in_specs=(rows, rows, rows, rows, P(), P(), P("groups")),
        out_specs=(rows, rows, rows),
        check_vma=False,
    )
```

```python
import math

import jax
import jax.numpy as jnp
from jax import lax
from jax.experimental import pallas as pl
from jax.experimental.pallas import tpu as pltpu
from jax.sharding import PartitionSpec as P

STEP = 16
WINDOW = 16
FIRST = (14, 15, 12, 13, 10, 11, 8, 9, 0, 1, 2, 3, 4, 5, 6, 7)
SECOND = (0, 1, 14, 15, 12, 13, 10, 11, 8, 9, 2, 3, 4, 5, 6, 7)
HALF = 128
FLOOR = -1e30
LOG2E = 1.4426950408889634
EARLY_HEADS = 8
VMEM_LIMIT = 48 * 2**20

BF = jnp.bfloat16
F32 = jnp.float32


def nn(a, b):
    return lax.dot_general(a, b, (((1,), (0,)), ((), ())), preferred_element_type=F32)


def nt(a, b):
    return lax.dot_general(a, b, (((1,), (1,)), ((), ())), preferred_element_type=F32)


def tn(a, b):
    return lax.dot_general(a, b, (((0,), (0,)), ((), ())), preferred_element_type=F32)


def parts_of(x, count):
    out = []
    for _ in range(count - 1):
        head = x.astype(BF).astype(F32)
        out.append(head)
        x = x - head
    out.append(x)
    return out


def rows_block(rows, height, width):
    at = lax.broadcasted_iota(jnp.int32, (height, width), 0)
    block = jnp.zeros((height, width), F32)
    for n, row in enumerate(rows):
        block = jnp.where(at == n, row, block)
    return block


def gather_rows(at, *counts):
    row = lax.broadcasted_iota(jnp.int32, (16, HALF), 0)
    lane = lax.broadcasted_iota(jnp.int32, (16, HALF), 1)
    total = jnp.zeros((16, HALF), F32)
    for n, count in enumerate(counts):
        hit = (row == n) & (lane >= at) & (lane < at + count)
        total = jnp.where(hit, 1.0, total)
        at += count
    return total.astype(BF)


def kernel(
    span_hbm, res_hbm, count_hbm, q_hbm, k_hbm, v_hbm, g_hbm,
    dq_ref, dk_ref, dv_ref, back_ref, pb, dpb, qb, gb, k_ref, here_ref,
    q_ref, v_ref, g_ref, load_sem, qt, kt, vt, gt, dqt, dkt, dvt, pick, far, w_ref, ds_ref,
    send1, recv1, send2, recv2, ss1, rs1, ss2, rs2, span_ref, res_ref, count_ref, small_sem,
):
    tokens, width = q_ref.shape
    heads = span_hbm.shape[0]
    dim = width // heads
    few = tokens // STEP
    chosen = heads * few
    scale = 1.0 / math.sqrt(dim)
    scale2 = scale * LOG2E
    me = lax.axis_index("seq")
    base = (me // WINDOW) * WINDOW
    my = me - base
    barrier = pltpu.get_barrier_semaphore()
    bits = [lax.rem(my // b, 2) for b in (1, 2, 4, 8)]
    for n in range(WINDOW - 1, 0, -1):
        to = my
        for at, b in enumerate((1, 2, 4, 8)):
            if n & b:
                to = to + b - 2 * b * bits[at]
        pl.semaphore_signal(
            barrier, inc=1, device_id={"seq": base + to},
            device_id_type=pl.DeviceIdType.MESH,
        )

    smalls = [
        pltpu.make_async_copy(source, target, small_sem.at[n])
        for n, (source, target) in enumerate(
            ((count_hbm, count_ref), (span_hbm, span_ref), (res_hbm, res_ref))
        )
    ]
    for small in smalls:
        small.start()
    loads = [
        pltpu.make_async_copy(source, target, load_sem.at[n])
        for n, (source, target) in enumerate(
            ((q_hbm, q_ref), (g_hbm, g_ref), (k_hbm, k_ref), (v_hbm, v_ref))
        )
    ]
    for load in loads:
        load.start()

    def block_of(n):
        return pl.ds(pl.multiple_of(n * few, few), few)

    def send_to(to, source, target, send_sem, recv_sem):
        return pltpu.make_async_remote_copy(
            src_ref=source.at[pl.ds(to * few, few)],
            dst_ref=target.at[block_of(my)],
            send_sem=send_sem,
            recv_sem=recv_sem,
            device_id={"seq": base + to},
            device_id_type=pl.DeviceIdType.MESH,
        )

    def start_all(order, *args):
        for to in order:
            @pl.when(my != to)
            def _():
                send_to(to, *args).start()

    def all_of(source, target, send_sem, recv_sem):
        others = pl.ds(0, (WINDOW - 1) * few)
        return pltpu.make_async_remote_copy(
            src_ref=source.at[others],
            dst_ref=target.at[others],
            send_sem=send_sem,
            recv_sem=recv_sem,
            device_id={"seq": base + lax.rem(my + 1, WINDOW)},
            device_id_type=pl.DeviceIdType.MESH,
        )

    def wait_all(*args):
        all_of(*args).wait_recv()

    def wait_sent(*args):
        all_of(*args).wait_send()

    for small in smalls:
        small.wait()
    count = count_ref[0]
    lane = lax.broadcasted_iota(jnp.int32, (1, chosen), 1)
    lane_head = lane // few
    lane_res = jnp.zeros((1, chosen), jnp.int32)
    lane_span = jnp.zeros((1, chosen), jnp.int32)
    for h in range(heads):
        lane_res = jnp.where(lane_head == h, res_ref[h], lane_res)
        lane_span = jnp.where(lane_head == h, span_ref[h], lane_span)
    lane_token = (lane % few) * STEP + lane_res
    row = lax.broadcasted_iota(jnp.int32, (tokens, tokens), 0)
    col = lax.broadcasted_iota(jnp.int32, (tokens, tokens), 1)
    start = me * tokens
    huge = jnp.int32(1 << 20)
    row_ok = row + start < count
    far[...] = jnp.where(row_ok, row ^ col, huge)
    pick[...] = (row == lane_token).astype(F32).astype(BF)

    for load, source, target in zip(
        loads, (q_ref, g_ref, k_ref, v_ref), (qt, gt, kt, vt)
    ):
        load.wait()
        target[...] = source[...].T

    def picked(source, keep):
        full = nn(source[...], pick[...])
        total = jnp.zeros((dim, chosen), F32)
        for h in range(heads):
            part = jnp.where(lane_head == h, full[h * dim : (h + 1) * dim], 0.0)
            if keep is not None:
                keep[h * dim : (h + 1) * dim, :] = part.astype(BF)
            total = total + part
        return total

    q_few = picked(qt, qb)
    g_few = picked(gt, gb)
    k_few = picked(kt, None)
    v_few = picked(vt, None)

    mask = jnp.where(row_ok, row ^ lane_token, huge) < lane_span
    s = jnp.where(mask, nn(k_ref[...], qb[...]) * scale2, FLOOR)
    top = jnp.max(s, axis=0, keepdims=True)
    p = jnp.exp2(s - top)
    total = jnp.sum(p, axis=0, keepdims=True)
    p = p * (1.0 / total)
    dp = nn(v_ref[...], gb[...])
    local_lse = top + jnp.log(total) * LOG2E
    local_delta = jnp.sum(p * dp, axis=0, keepdims=True)
    pb[...] = p
    dpb[...] = dp
    gap = HALF // 2 - dim
    stats = rows_block(parts_of(local_lse, 3) + parts_of(local_delta, 2), gap, chosen)
    blank = jnp.zeros((gap, chosen), F32)
    packed = jnp.concatenate(
        [q_few, stats, v_few, blank, k_few, blank, g_few, blank], axis=0
    )
    send1[...] = packed.T.astype(BF)

    pl.semaphore_wait(barrier, WINDOW - 1)
    start_all(FIRST, send1, recv1, ss1, rs1)
    recv1[block_of(my), :] = send1[block_of(my), :]

    query_ok = lane + start < count

    def head_at(h):
        return pl.ds(pl.multiple_of(h * dim, 16), dim)

    def weigh(h, slot):
        at = head_at(h)
        qh, kh, vh, gh = qt[at, :], kt[at, :], vt[at, :], gt[at, :]
        s = jnp.where(far[...] < span_ref[h], tn(kh, qh) * scale2, FLOOR)
        top = jnp.max(s, axis=0, keepdims=True)
        p = jnp.exp2(s - top)
        inverse = 1.0 / jnp.sum(p, axis=0, keepdims=True)
        dp = tn(vh, gh)
        delta = jnp.sum(p * dp, axis=0, keepdims=True) * inverse
        keep = query_ok & (lane % STEP != res_ref[h])
        w = p * jnp.where(keep, inverse, 0.0)
        w_ref[slot] = w.astype(BF)
        ds_ref[slot] = (w * (dp - delta)).astype(BF)

    def gather(h, slot):
        at = head_at(h)
        dqt[at, :] = nn(kt[at, :], ds_ref[slot]) * scale
        dkt[at, :] = nt(qt[at, :], ds_ref[slot]) * scale
        dvt[at, :] = nt(gt[at, :], w_ref[slot])

    def local_heads(first, last):
        weigh(first, 0)
        weigh(first + 1, 1)

        def pair(n, carry):
            h = first + 2 * n
            gather(h - 2, 0)
            weigh(h, 0)
            gather(h - 1, 1)
            weigh(h + 1, 1)
            return carry

        lax.fori_loop(1, (last - first) // 2, pair, 0)
        gather(last - 2, 0)
        gather(last - 1, 1)

    local_heads(0, EARLY_HEADS)

    wait_all(send1, recv1, ss1, rs1)
    at = lax.broadcasted_iota(jnp.int32, (1, HALF), 1)
    low = at < HALF // 2
    first = jnp.where(at < dim, 1.0, 0.0).astype(BF)
    second = jnp.where((at >= HALF // 2) & (at < HALF // 2 + dim), 1.0, 0.0).astype(BF)
    left, right = recv1[:, :HALF], recv1[:, HALF:]
    limit = count - base * tokens - res_ref[my]
    s = jnp.where(row * STEP < limit, nt(right * first, left) * scale2, FLOOR)
    stats = nt(gather_rows(dim, 3, 2), left)
    local_lse, local_delta = stats[0:1], stats[1:2]
    dp = nt(left * second, right)
    top = jnp.max(s, axis=0, keepdims=True)
    p = jnp.exp2(s - top)
    total = jnp.sum(p, axis=0, keepdims=True)
    dilated_lse = top + jnp.log(total) * LOG2E
    most = jnp.maximum(local_lse, dilated_lse)
    both = most + jnp.log(jnp.exp2(local_lse - most) + jnp.exp2(dilated_lse - most)) * LOG2E
    here_ok = lane * STEP < limit
    local_part = jnp.where(here_ok, jnp.exp2(local_lse - both), 0.0)
    u = p * jnp.where(here_ok, jnp.exp2(top - both), 0.0)
    delta = local_part * local_delta + jnp.sum(u * dp, axis=0, keepdims=True)
    delta = jnp.where(here_ok, delta, 0.0)
    ds = (u * (dp - delta)).astype(BF)
    stats = rows_block(parts_of(local_part, 2) + parts_of(delta, 2), 16, chosen)
    dk_dv = jnp.where(low, nn(ds, left) * scale, nn(u.astype(BF), right))
    send2[:, :HALF] = dk_dv.astype(BF)
    place = lax.broadcasted_iota(jnp.int32, (16, HALF), 0) + HALF // 2
    place = (place == lax.broadcasted_iota(jnp.int32, (16, HALF), 1)).astype(F32)
    dq_stats = jnp.where(low, tn(ds, right) * scale, tn(stats.astype(BF), place.astype(BF)))
    send2[:, HALF:] = dq_stats.astype(BF)
    start_all(SECOND, send2, recv2, ss2, rs2)
    recv2[block_of(my), :] = send2[block_of(my), :]

    local_heads(EARLY_HEADS, heads)

    dq_ref[...] = dqt[...].T
    dk_ref[...] = dkt[...].T
    dv_ref[...] = dvt[...].T
    wide = lax.broadcasted_iota(jnp.int32, (STEP, width), 1)
    wide_res = jnp.zeros((STEP, width), jnp.int32)
    for h in range(heads):
        wide_res = jnp.where(wide >= h * dim, res_ref[h], wide_res)
    at = lax.broadcasted_iota(jnp.int32, (STEP, width), 0)
    here_ref[...] = (at == wide_res).astype(F32)

    wait_all(send2, recv2, ss2, rs2)
    back_ref[...] = recv2[...]
    wait_sent(send1, recv1, ss1, rs1)
    wait_sent(send2, recv2, ss2, rs2)


def finish(
    dq_in, dk_in, dv_in, back, pb, dpb, qb, gb, k_ref, here,
    dq_hbm, dk_hbm, dv_hbm, staged, few, ds_ref, w_ref, store_sem,
):
    tokens, width = dq_in.shape
    chosen = pb.shape[1]
    heads = chosen // STEP
    dim = width // heads
    scale = 1.0 / math.sqrt(dim)
    half, lanes = chosen // 2, width // 2
    stats = nt(gather_rows(HALF // 2, 2, 2), back[:, HALF:])
    w = pb[...] * stats[0:1]
    w_ref[...] = w.astype(BF)
    ds_ref[...] = (w * ((dpb[...] - stats[1:2]) * scale)).astype(BF)
    at = lax.broadcasted_iota(jnp.int32, (STEP, HALF), 1)

    def tiles_of(h):
        first = h * dim // HALF
        return range(first, (h * dim + dim - 1) // HALF + 1)

    def gathered(piece_of):
        tiles = [jnp.zeros((STEP, HALF), F32) for _ in range(width // HALF)]
        for h in range(heads):
            for n in tiles_of(h):
                start = h * dim - n * HALF
                here_too = (at >= start) & (at < start + dim)
                tiles[n] = jnp.where(here_too, piece_of(h, n), tiles[n])
        return jnp.concatenate(tiles, axis=1)

    def sent(column, start):
        def piece(h, n):
            block = back[h * STEP : (h + 1) * STEP, column * HALF : (column + 1) * HALF]
            return pltpu.roll(block.astype(F32), (h * dim - start) % HALF, axis=1)

        return piece

    def emit(n, source, product, target):
        for t in range(tokens // STEP):
            rows = slice(t * STEP, (t + 1) * STEP)
            value = source[rows] + here[...] * few[n, t : t + 1, :]
            if product is not None:
                value = value + product[rows]
            staged[n, rows] = value.astype(BF)
        copy = pltpu.make_async_copy(staged.at[n], target, store_sem.at[n])
        copy.start()
        return copy

    few[0] = gathered(sent(0, HALF // 2))
    few[1] = gathered(sent(0, 0))
    store_dv = emit(0, dv_in, nt(w_ref[...], gb[...]), dv_hbm)
    store_dk = emit(1, dk_in, nt(ds_ref[...], qb[...]), dk_hbm)
    own = [
        tn(ds_ref[:, n * half : (n + 1) * half], k_ref[:, n * lanes : (n + 1) * lanes])
        for n in range(2)
    ]

    def own_piece(h, n):
        side = h * STEP // half
        block = own[side][h * STEP - side * half : (h + 1) * STEP - side * half]
        block = block[:, n * HALF - side * lanes : (n + 1) * HALF - side * lanes]
        return block + sent(1, 0)(h, n)

    few[2] = gathered(own_piece)
    store_dq = emit(2, dq_in, None, dq_hbm)
    store_dv.wait()
    store_dk.wait()
    store_dq.wait()


def in_hbm(x):
    return pltpu.with_memory_space_constraint(x, pltpu.MemorySpace.HBM)


def shards(queries, keys, values, grad_out, local_span, head_residue, valid_count):
    tokens, width = queries.shape
    heads = local_span.shape[0]
    chosen = heads * (tokens // STEP)
    assert heads == WINDOW and chosen == tokens
    vmem = pl.BlockSpec(memory_space=pltpu.VMEM)
    hbm = pl.BlockSpec(memory_space=pltpu.MemorySpace.HBM)
    out = jax.ShapeDtypeStruct((tokens, width), BF)
    full = pltpu.VMEM((tokens, width), F32)
    passed = pl.pallas_call(
        kernel,
        out_shape=(full, full, full)
        + (
            pltpu.VMEM((chosen, chosen), BF),
            pltpu.VMEM((tokens, chosen), F32),
            pltpu.VMEM((tokens, chosen), F32),
            pltpu.VMEM((width, chosen), BF),
            pltpu.VMEM((width, chosen), BF),
            pltpu.VMEM((tokens, width), BF),
            pltpu.VMEM((STEP, width), F32),
        ),
        in_specs=[hbm] * 7,
        out_specs=(vmem,) * 10,
        scratch_shapes=[pltpu.VMEM((tokens, width), BF)] * 3
        + [pltpu.SemaphoreType.DMA((4,))]
        + [pltpu.VMEM((width, tokens), BF)] * 4
        + [pltpu.VMEM((width, tokens), F32)] * 3
        + [
            pltpu.VMEM((tokens, chosen), BF),
            pltpu.VMEM((tokens, tokens), jnp.int32),
            pltpu.VMEM((2, tokens, tokens), BF),
            pltpu.VMEM((2, tokens, tokens), BF),
        ]
        + [pltpu.VMEM((chosen, chosen), BF)] * 4
        + [pltpu.SemaphoreType.DMA] * 4
        + [pltpu.SMEM((heads,), jnp.int32)] * 2
        + [pltpu.SMEM((1,), jnp.int32), pltpu.SemaphoreType.DMA((3,))],
        compiler_params=pltpu.CompilerParams(
            collective_id=0, has_side_effects=True, vmem_limit_bytes=VMEM_LIMIT
        ),
    )(
        *[in_hbm(x) for x in (local_span, head_residue)],
        valid_count,
        *[in_hbm(x) for x in (queries, keys, values, grad_out)],
    )
    return pl.pallas_call(
        finish,
        out_shape=(out, out, out),
        in_specs=[vmem] * 10,
        out_specs=(hbm, hbm, hbm),
        scratch_shapes=[
            pltpu.VMEM((3, tokens, width), BF),
            pltpu.VMEM((3, STEP, width), F32),
            pltpu.VMEM((tokens, chosen), BF),
            pltpu.VMEM((tokens, chosen), BF),
            pltpu.SemaphoreType.DMA((3,)),
        ],
        compiler_params=pltpu.CompilerParams(vmem_limit_bytes=VMEM_LIMIT),
    )(*[pltpu.with_memory_space_constraint(x, pltpu.MemorySpace.VMEM) for x in passed])


def solution(mesh):
    rows = P(("groups", "seq"), None)
    return jax.shard_map(
        shards,
        mesh=mesh,
        in_specs=(rows, rows, rows, rows, P(), P(), P("groups")),
        out_specs=(rows, rows, rows),
        check_vma=False,
    )
```

```python
import math

import jax
import jax.numpy as jnp
from jax import lax
from jax.experimental import pallas as pl
from jax.experimental.pallas import tpu as pltpu
from jax.sharding import PartitionSpec as P

STEP = 16
WINDOW = 16
FIRST = (14, 15, 12, 13, 10, 11, 8, 9, 0, 1, 2, 3, 4, 5, 6, 7)
SECOND = (0, 1, 14, 15, 12, 13, 10, 11, 8, 9, 2, 3, 4, 5, 6, 7)
HALF = 128
FLOOR = -1e30
LOG2E = 1.4426950408889634
EARLY_HEADS = 8
VMEM_LIMIT = 48 * 2**20

BF = jnp.bfloat16
F32 = jnp.float32


def nn(a, b):
    return lax.dot_general(a, b, (((1,), (0,)), ((), ())), preferred_element_type=F32)


def nt(a, b):
    return lax.dot_general(a, b, (((1,), (1,)), ((), ())), preferred_element_type=F32)


def tn(a, b):
    return lax.dot_general(a, b, (((0,), (0,)), ((), ())), preferred_element_type=F32)


def parts_of(x, count):
    out = []
    for _ in range(count - 1):
        head = x.astype(BF).astype(F32)
        out.append(head)
        x = x - head
    out.append(x)
    return out


def rows_block(rows, height, width):
    at = lax.broadcasted_iota(jnp.int32, (height, width), 0)
    block = jnp.zeros((height, width), F32)
    for n, row in enumerate(rows):
        block = jnp.where(at == n, row, block)
    return block


def gather_rows(at, *counts):
    row = lax.broadcasted_iota(jnp.int32, (16, HALF), 0)
    lane = lax.broadcasted_iota(jnp.int32, (16, HALF), 1)
    total = jnp.zeros((16, HALF), F32)
    for n, count in enumerate(counts):
        hit = (row == n) & (lane >= at) & (lane < at + count)
        total = jnp.where(hit, 1.0, total)
        at += count
    return total.astype(BF)


def kernel(
    span_hbm, res_hbm, count_hbm, q_hbm, k_hbm, v_hbm, g_hbm,
    dq_ref, dk_ref, dv_ref, back_ref, pb, dpb, qb, gb, k_ref, here_ref,
    q_ref, v_ref, g_ref, load_sem, qt, kt, vt, gt, dqt, dkt, dvt, pick, far, w_ref, ds_ref,
    send1, recv1, send2, ss1, rs1, ss2, rs2, span_ref, res_ref, count_ref, small_sem,
):
    tokens, width = q_ref.shape
    heads = span_hbm.shape[0]
    dim = width // heads
    few = tokens // STEP
    chosen = heads * few
    scale = 1.0 / math.sqrt(dim)
    scale2 = scale * LOG2E
    me = lax.axis_index("seq")
    base = (me // WINDOW) * WINDOW
    my = me - base
    barrier = pltpu.get_barrier_semaphore()
    bits = [lax.rem(my // b, 2) for b in (1, 2, 4, 8)]
    for n in range(WINDOW - 1, 0, -1):
        to = my
        for at, b in enumerate((1, 2, 4, 8)):
            if n & b:
                to = to + b - 2 * b * bits[at]
        pl.semaphore_signal(
            barrier, inc=1, device_id={"seq": base + to},
            device_id_type=pl.DeviceIdType.MESH,
        )

    smalls = [
        pltpu.make_async_copy(source, target, small_sem.at[n])
        for n, (source, target) in enumerate(
            ((count_hbm, count_ref), (span_hbm, span_ref), (res_hbm, res_ref))
        )
    ]
    for small in smalls:
        small.start()
    loads = [
        pltpu.make_async_copy(source, target, load_sem.at[n])
        for n, (source, target) in enumerate(
            ((q_hbm, q_ref), (g_hbm, g_ref), (k_hbm, k_ref), (v_hbm, v_ref))
        )
    ]
    for load in loads:
        load.start()

    def block_of(n):
        return pl.ds(pl.multiple_of(n * few, few), few)

    def send_to(to, source, target, send_sem, recv_sem):
        return pltpu.make_async_remote_copy(
            src_ref=source.at[pl.ds(to * few, few)],
            dst_ref=target.at[block_of(my)],
            send_sem=send_sem,
            recv_sem=recv_sem,
            device_id={"seq": base + to},
            device_id_type=pl.DeviceIdType.MESH,
        )

    def start_all(order, *args):
        for to in order:
            @pl.when(my != to)
            def _():
                send_to(to, *args).start()

    def all_of(source, target, send_sem, recv_sem):
        others = pl.ds(0, (WINDOW - 1) * few)
        return pltpu.make_async_remote_copy(
            src_ref=source.at[others],
            dst_ref=target.at[others],
            send_sem=send_sem,
            recv_sem=recv_sem,
            device_id={"seq": base + lax.rem(my + 1, WINDOW)},
            device_id_type=pl.DeviceIdType.MESH,
        )

    def wait_all(*args):
        all_of(*args).wait_recv()

    def wait_sent(*args):
        all_of(*args).wait_send()

    for small in smalls:
        small.wait()
    count = count_ref[0]
    lane = lax.broadcasted_iota(jnp.int32, (1, chosen), 1)
    lane_head = lane // few
    lane_res = jnp.zeros((1, chosen), jnp.int32)
    lane_span = jnp.zeros((1, chosen), jnp.int32)
    for h in range(heads):
        lane_res = jnp.where(lane_head == h, res_ref[h], lane_res)
        lane_span = jnp.where(lane_head == h, span_ref[h], lane_span)
    lane_token = (lane % few) * STEP + lane_res
    row = lax.broadcasted_iota(jnp.int32, (tokens, tokens), 0)
    col = lax.broadcasted_iota(jnp.int32, (tokens, tokens), 1)
    start = me * tokens
    huge = jnp.int32(1 << 20)
    row_ok = row + start < count
    far[...] = jnp.where(row_ok, row ^ col, huge)
    pick[...] = (row == lane_token).astype(F32).astype(BF)

    for load, source, target in zip(
        loads, (q_ref, g_ref, k_ref, v_ref), (qt, gt, kt, vt)
    ):
        load.wait()
        target[...] = source[...].T

    def picked(source, keep):
        full = nn(source[...], pick[...])
        total = jnp.zeros((dim, chosen), F32)
        for h in range(heads):
            part = jnp.where(lane_head == h, full[h * dim : (h + 1) * dim], 0.0)
            if keep is not None:
                keep[h * dim : (h + 1) * dim, :] = part.astype(BF)
            total = total + part
        return total

    q_few = picked(qt, qb)
    g_few = picked(gt, gb)
    k_few = picked(kt, None)
    v_few = picked(vt, None)

    mask = jnp.where(row_ok, row ^ lane_token, huge) < lane_span
    s = jnp.where(mask, nn(k_ref[...], qb[...]) * scale2, FLOOR)
    top = jnp.max(s, axis=0, keepdims=True)
    p = jnp.exp2(s - top)
    total = jnp.sum(p, axis=0, keepdims=True)
    p = p * (1.0 / total)
    dp = nn(v_ref[...], gb[...])
    local_lse = top + jnp.log(total) * LOG2E
    local_delta = jnp.sum(p * dp, axis=0, keepdims=True)
    pb[...] = p
    dpb[...] = dp
    gap = HALF // 2 - dim
    stats = rows_block(parts_of(local_lse, 3) + parts_of(local_delta, 2), gap, chosen)
    blank = jnp.zeros((gap, chosen), F32)
    packed = jnp.concatenate(
        [q_few, stats, v_few, blank, k_few, blank, g_few, blank], axis=0
    )
    send1[...] = packed.T.astype(BF)

    pl.semaphore_wait(barrier, WINDOW - 1)
    start_all(FIRST, send1, recv1, ss1, rs1)
    recv1[block_of(my), :] = send1[block_of(my), :]

    query_ok = lane + start < count

    def head_at(h):
        return pl.ds(pl.multiple_of(h * dim, 16), dim)

    def weigh(h, slot):
        at = head_at(h)
        qh, kh, vh, gh = qt[at, :], kt[at, :], vt[at, :], gt[at, :]
        s = jnp.where(far[...] < span_ref[h], tn(kh, qh) * scale2, FLOOR)
        top = jnp.max(s, axis=0, keepdims=True)
        p = jnp.exp2(s - top)
        inverse = 1.0 / jnp.sum(p, axis=0, keepdims=True)
        dp = tn(vh, gh)
        delta = jnp.sum(p * dp, axis=0, keepdims=True) * inverse
        keep = query_ok & (lane % STEP != res_ref[h])
        w = p * jnp.where(keep, inverse, 0.0)
        w_ref[slot] = w.astype(BF)
        ds_ref[slot] = (w * (dp - delta)).astype(BF)

    def gather(h, slot):
        at = head_at(h)
        dqt[at, :] = nn(kt[at, :], ds_ref[slot]) * scale
        dkt[at, :] = nt(qt[at, :], ds_ref[slot]) * scale
        dvt[at, :] = nt(gt[at, :], w_ref[slot])

    def local_heads(first, last):
        weigh(first, 0)
        weigh(first + 1, 1)

        def pair(n, carry):
            h = first + 2 * n
            gather(h - 2, 0)
            weigh(h, 0)
            gather(h - 1, 1)
            weigh(h + 1, 1)
            return carry

        lax.fori_loop(1, (last - first) // 2, pair, 0)
        gather(last - 2, 0)
        gather(last - 1, 1)

    local_heads(0, EARLY_HEADS)

    wait_all(send1, recv1, ss1, rs1)
    at = lax.broadcasted_iota(jnp.int32, (1, HALF), 1)
    low = at < HALF // 2
    first = jnp.where(at < dim, 1.0, 0.0).astype(BF)
    second = jnp.where((at >= HALF // 2) & (at < HALF // 2 + dim), 1.0, 0.0).astype(BF)
    left, right = recv1[:, :HALF], recv1[:, HALF:]
    limit = count - base * tokens - res_ref[my]
    rows_left = (limit + STEP - 1) // STEP
    s = jnp.where(row < rows_left, nt(right * first, left) * scale2, FLOOR)
    stats = nt(gather_rows(dim, 3, 2), left)
    local_lse, local_delta = stats[0:1], stats[1:2]
    dp = nt(left * second, right)
    top = jnp.max(s, axis=0, keepdims=True)
    p = jnp.exp2(s - top)
    total = jnp.sum(p, axis=0, keepdims=True)
    dilated_lse = top + jnp.log(total) * LOG2E
    most = jnp.maximum(local_lse, dilated_lse)
    both = most + jnp.log(jnp.exp2(local_lse - most) + jnp.exp2(dilated_lse - most)) * LOG2E
    here_ok = lane * STEP < limit
    local_part = jnp.where(here_ok, jnp.exp2(local_lse - both), 0.0)
    u = p * jnp.where(here_ok, jnp.exp2(top - both), 0.0)
    delta = local_part * local_delta + jnp.sum(u * dp, axis=0, keepdims=True)
    delta = jnp.where(here_ok, delta, 0.0)
    ds = (u * (dp - delta)).astype(BF)
    stats = rows_block(parts_of(local_part, 2) + parts_of(delta, 2), 16, chosen)
    dk_dv = jnp.where(low, nn(ds, left) * scale, nn(u.astype(BF), right))
    send2[:, :HALF] = dk_dv.astype(BF)
    place = lax.broadcasted_iota(jnp.int32, (16, HALF), 0) + HALF // 2
    place = (place == lax.broadcasted_iota(jnp.int32, (16, HALF), 1)).astype(F32)
    dq_stats = jnp.where(low, tn(ds, right) * scale, tn(stats.astype(BF), place.astype(BF)))
    send2[:, HALF:] = dq_stats.astype(BF)
    start_all(SECOND, send2, back_ref, ss2, rs2)
    back_ref[block_of(my), :] = send2[block_of(my), :]

    local_heads(EARLY_HEADS, heads)

    dq_ref[...] = dqt[...].T
    dk_ref[...] = dkt[...].T
    dv_ref[...] = dvt[...].T
    wide = lax.broadcasted_iota(jnp.int32, (STEP, width), 1)
    wide_res = jnp.zeros((STEP, width), jnp.int32)
    for h in range(heads):
        wide_res = jnp.where(wide >= h * dim, res_ref[h], wide_res)
    at = lax.broadcasted_iota(jnp.int32, (STEP, width), 0)
    here_ref[...] = (at == wide_res).astype(F32)

    wait_all(send2, back_ref, ss2, rs2)
    wait_sent(send1, recv1, ss1, rs1)
    wait_sent(send2, back_ref, ss2, rs2)


def finish(
    dq_in, dk_in, dv_in, back, pb, dpb, qb, gb, k_ref, here,
    dq_hbm, dk_hbm, dv_hbm, staged, few, ds_ref, w_ref, store_sem,
):
    tokens, width = dq_in.shape
    chosen = pb.shape[1]
    heads = chosen // STEP
    dim = width // heads
    scale = 1.0 / math.sqrt(dim)
    half, lanes = chosen // 2, width // 2
    stats = nt(gather_rows(HALF // 2, 2, 2), back[:, HALF:])
    w = pb[...] * stats[0:1]
    w_ref[...] = w.astype(BF)
    ds_ref[...] = (w * ((dpb[...] - stats[1:2]) * scale)).astype(BF)
    at = lax.broadcasted_iota(jnp.int32, (STEP, HALF), 1)

    def tiles_of(h):
        first = h * dim // HALF
        return range(first, (h * dim + dim - 1) // HALF + 1)

    def gathered(piece_of):
        tiles = [jnp.zeros((STEP, HALF), F32) for _ in range(width // HALF)]
        for h in range(heads):
            for n in tiles_of(h):
                start = h * dim - n * HALF
                here_too = (at >= start) & (at < start + dim)
                tiles[n] = jnp.where(here_too, piece_of(h, n), tiles[n])
        return jnp.concatenate(tiles, axis=1)

    def sent(column, start):
        def piece(h, n):
            block = back[h * STEP : (h + 1) * STEP, column * HALF : (column + 1) * HALF]
            return pltpu.roll(block.astype(F32), (h * dim - start) % HALF, axis=1)

        return piece

    def emit(n, source, factor, other, target):
        for start in range(0, width, chosen):
            part = slice(start, start + chosen)
            product = None if factor is None else nt(factor[...], other[part])
            for t in range(tokens // STEP):
                rows = slice(t * STEP, (t + 1) * STEP)
                value = source[rows, part] + here[:, part] * few[n, t : t + 1, part]
                if product is not None:
                    value = value + product[rows]
                staged[n, rows, part] = value.astype(BF)
        copy = pltpu.make_async_copy(staged.at[n], target, store_sem.at[n])
        copy.start()
        return copy

    few[0] = gathered(sent(0, HALF // 2))
    few[1] = gathered(sent(0, 0))
    store_dv = emit(0, dv_in, w_ref, gb, dv_hbm)
    store_dk = emit(1, dk_in, ds_ref, qb, dk_hbm)
    own = [
        tn(ds_ref[:, n * half : (n + 1) * half], k_ref[:, n * lanes : (n + 1) * lanes])
        for n in range(2)
    ]

    def own_piece(h, n):
        side = h * STEP // half
        block = own[side][h * STEP - side * half : (h + 1) * STEP - side * half]
        block = block[:, n * HALF - side * lanes : (n + 1) * HALF - side * lanes]
        return block + sent(1, 0)(h, n)

    few[2] = gathered(own_piece)
    store_dq = emit(2, dq_in, None, None, dq_hbm)
    store_dv.wait()
    store_dk.wait()
    store_dq.wait()


def in_hbm(x):
    return pltpu.with_memory_space_constraint(x, pltpu.MemorySpace.HBM)


def shards(queries, keys, values, grad_out, local_span, head_residue, valid_count):
    tokens, width = queries.shape
    heads = local_span.shape[0]
    chosen = heads * (tokens // STEP)
    assert heads == WINDOW and chosen == tokens
    vmem = pl.BlockSpec(memory_space=pltpu.VMEM)
    hbm = pl.BlockSpec(memory_space=pltpu.MemorySpace.HBM)
    out = jax.ShapeDtypeStruct((tokens, width), BF)
    full = pltpu.VMEM((tokens, width), F32)
    passed = pl.pallas_call(
        kernel,
        out_shape=(full, full, full)
        + (
            pltpu.VMEM((chosen, chosen), BF),
            pltpu.VMEM((tokens, chosen), F32),
            pltpu.VMEM((tokens, chosen), F32),
            pltpu.VMEM((width, chosen), BF),
            pltpu.VMEM((width, chosen), BF),
            pltpu.VMEM((tokens, width), BF),
            pltpu.VMEM((STEP, width), F32),
        ),
        in_specs=[hbm] * 7,
        out_specs=(vmem,) * 10,
        scratch_shapes=[pltpu.VMEM((tokens, width), BF)] * 3
        + [pltpu.SemaphoreType.DMA((4,))]
        + [pltpu.VMEM((width, tokens), BF)] * 4
        + [pltpu.VMEM((width, tokens), F32)] * 3
        + [
            pltpu.VMEM((tokens, chosen), BF),
            pltpu.VMEM((tokens, tokens), jnp.int32),
            pltpu.VMEM((2, tokens, tokens), BF),
            pltpu.VMEM((2, tokens, tokens), BF),
        ]
        + [pltpu.VMEM((chosen, chosen), BF)] * 3
        + [pltpu.SemaphoreType.DMA] * 4
        + [pltpu.SMEM((heads,), jnp.int32)] * 2
        + [pltpu.SMEM((1,), jnp.int32), pltpu.SemaphoreType.DMA((3,))],
        compiler_params=pltpu.CompilerParams(
            collective_id=0, has_side_effects=True, vmem_limit_bytes=VMEM_LIMIT
        ),
    )(
        *[in_hbm(x) for x in (local_span, head_residue)],
        valid_count,
        *[in_hbm(x) for x in (queries, keys, values, grad_out)],
    )
    return pl.pallas_call(
        finish,
        out_shape=(out, out, out),
        in_specs=[vmem] * 10,
        out_specs=(hbm, hbm, hbm),
        scratch_shapes=[
            pltpu.VMEM((3, tokens, width), BF),
            pltpu.VMEM((3, STEP, width), F32),
            pltpu.VMEM((tokens, chosen), BF),
            pltpu.VMEM((tokens, chosen), BF),
            pltpu.SemaphoreType.DMA((3,)),
        ],
        compiler_params=pltpu.CompilerParams(vmem_limit_bytes=VMEM_LIMIT),
    )(*[pltpu.with_memory_space_constraint(x, pltpu.MemorySpace.VMEM) for x in passed])


def solution(mesh):
    rows = P(("groups", "seq"), None)
    return jax.shard_map(
        shards,
        mesh=mesh,
        in_specs=(rows, rows, rows, rows, P(), P(), P("groups")),
        out_specs=(rows, rows, rows),
        check_vma=False,
    )
```

```python
import math

import jax
import jax.numpy as jnp
from jax import lax
from jax.experimental import pallas as pl
from jax.experimental.pallas import tpu as pltpu
from jax.sharding import PartitionSpec as P

STEP = 16
WINDOW = 16
FIRST = (14, 12, 10, 8, 15, 13, 11, 9, 0, 2, 4, 6, 1, 3, 5, 7)
SECOND = (0, 1, 14, 12, 10, 8, 15, 13, 11, 9, 2, 4, 6, 3, 5, 7)
HALF = 128
FLOOR = -1e30
LOG2E = 1.4426950408889634
EARLY_HEADS = 8
VMEM_LIMIT = 48 * 2**20

BF = jnp.bfloat16
F32 = jnp.float32


def nn(a, b):
    return lax.dot_general(a, b, (((1,), (0,)), ((), ())), preferred_element_type=F32)


def nt(a, b):
    return lax.dot_general(a, b, (((1,), (1,)), ((), ())), preferred_element_type=F32)


def tn(a, b):
    return lax.dot_general(a, b, (((0,), (0,)), ((), ())), preferred_element_type=F32)


def parts_of(x, count):
    out = []
    for _ in range(count - 1):
        head = x.astype(BF).astype(F32)
        out.append(head)
        x = x - head
    out.append(x)
    return out


def rows_block(rows, height, width):
    at = lax.broadcasted_iota(jnp.int32, (height, width), 0)
    block = jnp.zeros((height, width), F32)
    for n, row in enumerate(rows):
        block = jnp.where(at == n, row, block)
    return block


def gather_rows(at, *counts):
    row = lax.broadcasted_iota(jnp.int32, (16, HALF), 0)
    lane = lax.broadcasted_iota(jnp.int32, (16, HALF), 1)
    total = jnp.zeros((16, HALF), F32)
    for n, count in enumerate(counts):
        hit = (row == n) & (lane >= at) & (lane < at + count)
        total = jnp.where(hit, 1.0, total)
        at += count
    return total.astype(BF)


def kernel(
    span_hbm, res_hbm, count_hbm, q_hbm, k_hbm, v_hbm, g_hbm,
    dq_ref, dk_ref, dv_ref, back_ref, pb, dpb, qb, gb, k_ref, here_ref,
    q_ref, v_ref, g_ref, load_sem, qt, kt, vt, gt, dqt, dkt, dvt, pick, far, w_ref, ds_ref,
    send1, recv1, send2, ss1, rs1, ss2, rs2, span_ref, res_ref, count_ref, small_sem,
):
    tokens, width = q_ref.shape
    heads = span_hbm.shape[0]
    dim = width // heads
    few = tokens // STEP
    chosen = heads * few
    scale = 1.0 / math.sqrt(dim)
    scale2 = scale * LOG2E
    me = lax.axis_index("seq")
    base = (me // WINDOW) * WINDOW
    my = me - base
    barrier = pltpu.get_barrier_semaphore()
    bits = [lax.rem(my // b, 2) for b in (1, 2, 4, 8)]
    for n in range(WINDOW - 1, 0, -1):
        to = my
        for at, b in enumerate((1, 2, 4, 8)):
            if n & b:
                to = to + b - 2 * b * bits[at]
        pl.semaphore_signal(
            barrier, inc=1, device_id={"seq": base + to},
            device_id_type=pl.DeviceIdType.MESH,
        )

    smalls = [
        pltpu.make_async_copy(source, target, small_sem.at[n])
        for n, (source, target) in enumerate(
            ((count_hbm, count_ref), (span_hbm, span_ref), (res_hbm, res_ref))
        )
    ]
    for small in smalls:
        small.start()
    loads = [
        pltpu.make_async_copy(source, target, load_sem.at[n])
        for n, (source, target) in enumerate(
            ((q_hbm, q_ref), (g_hbm, g_ref), (k_hbm, k_ref), (v_hbm, v_ref))
        )
    ]
    for load in loads:
        load.start()

    def block_of(n):
        return pl.ds(pl.multiple_of(n * few, few), few)

    def send_to(to, source, target, send_sem, recv_sem):
        return pltpu.make_async_remote_copy(
            src_ref=source.at[pl.ds(to * few, few)],
            dst_ref=target.at[block_of(my)],
            send_sem=send_sem,
            recv_sem=recv_sem,
            device_id={"seq": base + to},
            device_id_type=pl.DeviceIdType.MESH,
        )

    def start_all(order, *args):
        for to in order:
            @pl.when(my != to)
            def _():
                send_to(to, *args).start()

    def all_of(source, target, send_sem, recv_sem):
        others = pl.ds(0, (WINDOW - 1) * few)
        return pltpu.make_async_remote_copy(
            src_ref=source.at[others],
            dst_ref=target.at[others],
            send_sem=send_sem,
            recv_sem=recv_sem,
            device_id={"seq": base + lax.rem(my + 1, WINDOW)},
            device_id_type=pl.DeviceIdType.MESH,
        )

    def wait_all(*args):
        all_of(*args).wait_recv()

    def wait_sent(*args):
        all_of(*args).wait_send()

    for small in smalls:
        small.wait()
    count = count_ref[0]
    lane = lax.broadcasted_iota(jnp.int32, (1, chosen), 1)
    lane_head = lane // few
    lane_res = jnp.zeros((1, chosen), jnp.int32)
    lane_span = jnp.zeros((1, chosen), jnp.int32)
    for h in range(heads):
        lane_res = jnp.where(lane_head == h, res_ref[h], lane_res)
        lane_span = jnp.where(lane_head == h, span_ref[h], lane_span)
    lane_token = (lane % few) * STEP + lane_res
    row = lax.broadcasted_iota(jnp.int32, (tokens, tokens), 0)
    col = lax.broadcasted_iota(jnp.int32, (tokens, tokens), 1)
    start = me * tokens
    huge = jnp.int32(1 << 20)
    row_ok = row + start < count
    far[...] = jnp.where(row_ok, row ^ col, huge)
    pick[...] = (row == lane_token).astype(F32).astype(BF)

    for load, source, target in zip(
        loads, (q_ref, g_ref, k_ref, v_ref), (qt, gt, kt, vt)
    ):
        load.wait()
        target[...] = source[...].T

    def picked(source, keep):
        full = nn(source[...], pick[...])
        total = jnp.zeros((dim, chosen), F32)
        for h in range(heads):
            part = jnp.where(lane_head == h, full[h * dim : (h + 1) * dim], 0.0)
            if keep is not None:
                keep[h * dim : (h + 1) * dim, :] = part.astype(BF)
            total = total + part
        return total

    q_few = picked(qt, qb)
    g_few = picked(gt, gb)
    k_few = picked(kt, None)
    v_few = picked(vt, None)

    mask = jnp.where(row_ok, row ^ lane_token, huge) < lane_span
    s = jnp.where(mask, nn(k_ref[...], qb[...]) * scale2, FLOOR)
    top = jnp.max(s, axis=0, keepdims=True)
    p = jnp.exp2(s - top)
    total = jnp.sum(p, axis=0, keepdims=True)
    p = p * (1.0 / total)
    dp = nn(v_ref[...], gb[...])
    local_lse = top + jnp.log(total) * LOG2E
    local_delta = jnp.sum(p * dp, axis=0, keepdims=True)
    pb[...] = p
    dpb[...] = dp
    gap = HALF // 2 - dim
    stats = rows_block(parts_of(local_lse, 3) + parts_of(local_delta, 2), gap, chosen)
    blank = jnp.zeros((gap, chosen), F32)
    packed = jnp.concatenate(
        [q_few, stats, v_few, blank, k_few, blank, g_few, blank], axis=0
    )
    send1[...] = packed.T.astype(BF)

    pl.semaphore_wait(barrier, WINDOW - 1)
    start_all(FIRST, send1, recv1, ss1, rs1)
    recv1[block_of(my), :] = send1[block_of(my), :]

    query_ok = lane + start < count

    def head_at(h):
        return pl.ds(pl.multiple_of(h * dim, 16), dim)

    def weigh(h, slot):
        at = head_at(h)
        qh, kh, vh, gh = qt[at, :], kt[at, :], vt[at, :], gt[at, :]
        s = jnp.where(far[...] < span_ref[h], tn(kh, qh) * scale2, FLOOR)
        top = jnp.max(s, axis=0, keepdims=True)
        p = jnp.exp2(s - top)
        inverse = 1.0 / jnp.sum(p, axis=0, keepdims=True)
        dp = tn(vh, gh)
        delta = jnp.sum(p * dp, axis=0, keepdims=True) * inverse
        keep = query_ok & (lane % STEP != res_ref[h])
        w = p * jnp.where(keep, inverse, 0.0)
        w_ref[slot] = w.astype(BF)
        ds_ref[slot] = (w * (dp - delta)).astype(BF)

    def gather(h, slot):
        at = head_at(h)
        dqt[at, :] = nn(kt[at, :], ds_ref[slot]) * scale
        dkt[at, :] = nt(qt[at, :], ds_ref[slot]) * scale
        dvt[at, :] = nt(gt[at, :], w_ref[slot])

    def local_heads(first, last):
        weigh(first, 0)
        weigh(first + 1, 1)

        def pair(n, carry):
            h = first + 2 * n
            gather(h - 2, 0)
            weigh(h, 0)
            gather(h - 1, 1)
            weigh(h + 1, 1)
            return carry

        lax.fori_loop(1, (last - first) // 2, pair, 0)
        gather(last - 2, 0)
        gather(last - 1, 1)

    local_heads(0, EARLY_HEADS)

    wait_all(send1, recv1, ss1, rs1)
    at = lax.broadcasted_iota(jnp.int32, (1, HALF), 1)
    low = at < HALF // 2
    first = jnp.where(at < dim, 1.0, 0.0).astype(BF)
    second = jnp.where((at >= HALF // 2) & (at < HALF // 2 + dim), 1.0, 0.0).astype(BF)
    left, right = recv1[:, :HALF], recv1[:, HALF:]
    limit = count - base * tokens - res_ref[my]
    rows_left = (limit + STEP - 1) // STEP
    s = jnp.where(row < rows_left, nt(right * first, left) * scale2, FLOOR)
    stats = nt(gather_rows(dim, 3, 2), left)
    local_lse, local_delta = stats[0:1], stats[1:2]
    dp = nt(left * second, right)
    top = jnp.max(s, axis=0, keepdims=True)
    p = jnp.exp2(s - top)
    total = jnp.sum(p, axis=0, keepdims=True)
    dilated_lse = top + jnp.log(total) * LOG2E
    most = jnp.maximum(local_lse, dilated_lse)
    both = most + jnp.log(jnp.exp2(local_lse - most) + jnp.exp2(dilated_lse - most)) * LOG2E
    here_ok = lane * STEP < limit
    local_part = jnp.where(here_ok, jnp.exp2(local_lse - both), 0.0)
    u = p * jnp.where(here_ok, jnp.exp2(top - both), 0.0)
    delta = local_part * local_delta + jnp.sum(u * dp, axis=0, keepdims=True)
    delta = jnp.where(here_ok, delta, 0.0)
    ds = (u * (dp - delta)).astype(BF)
    stats = rows_block(parts_of(local_part, 2) + parts_of(delta, 2), 16, chosen)
    dk_dv = jnp.where(low, nn(ds, left) * scale, nn(u.astype(BF), right))
    send2[:, :HALF] = dk_dv.astype(BF)
    place = lax.broadcasted_iota(jnp.int32, (16, HALF), 0) + HALF // 2
    place = (place == lax.broadcasted_iota(jnp.int32, (16, HALF), 1)).astype(F32)
    dq_stats = jnp.where(low, tn(ds, right) * scale, tn(stats.astype(BF), place.astype(BF)))
    send2[:, HALF:] = dq_stats.astype(BF)
    start_all(SECOND, send2, back_ref, ss2, rs2)
    back_ref[block_of(my), :] = send2[block_of(my), :]

    local_heads(EARLY_HEADS, heads)

    dq_ref[...] = dqt[...].T
    dk_ref[...] = dkt[...].T
    dv_ref[...] = dvt[...].T
    wide = lax.broadcasted_iota(jnp.int32, (STEP, width), 1)
    wide_res = jnp.zeros((STEP, width), jnp.int32)
    for h in range(heads):
        wide_res = jnp.where(wide >= h * dim, res_ref[h], wide_res)
    at = lax.broadcasted_iota(jnp.int32, (STEP, width), 0)
    here_ref[...] = (at == wide_res).astype(F32)

    wait_sent(send1, recv1, ss1, rs1)
    wait_all(send2, back_ref, ss2, rs2)
    wait_sent(send2, back_ref, ss2, rs2)


def finish(
    dq_in, dk_in, dv_in, back, pb, dpb, qb, gb, k_ref, here,
    dq_hbm, dk_hbm, dv_hbm, staged, few, ds_ref, w_ref, store_sem,
):
    tokens, width = dq_in.shape
    chosen = pb.shape[1]
    heads = chosen // STEP
    dim = width // heads
    scale = 1.0 / math.sqrt(dim)
    half, lanes = chosen // 2, width // 2
    stats = nt(gather_rows(HALF // 2, 2, 2), back[:, HALF:])
    w = pb[...] * stats[0:1]
    w_ref[...] = w.astype(BF)
    ds_ref[...] = (w * ((dpb[...] - stats[1:2]) * scale)).astype(BF)
    at = lax.broadcasted_iota(jnp.int32, (STEP, HALF), 1)

    def tiles_of(h):
        first = h * dim // HALF
        return range(first, (h * dim + dim - 1) // HALF + 1)

    def gathered(piece_of):
        tiles = [jnp.zeros((STEP, HALF), F32) for _ in range(width // HALF)]
        for h in range(heads):
            for n in tiles_of(h):
                start = h * dim - n * HALF
                here_too = (at >= start) & (at < start + dim)
                tiles[n] = jnp.where(here_too, piece_of(h, n), tiles[n])
        return jnp.concatenate(tiles, axis=1)

    def sent(column, start):
        def piece(h, n):
            block = back[h * STEP : (h + 1) * STEP, column * HALF : (column + 1) * HALF]
            return pltpu.roll(block.astype(F32), (h * dim - start) % HALF, axis=1)

        return piece

    def emit(n, source, factor, other, target):
        for start in range(0, width, chosen):
            part = slice(start, start + chosen)
            product = None if factor is None else nt(factor[...], other[part])
            for t in range(tokens // STEP):
                rows = slice(t * STEP, (t + 1) * STEP)
                value = source[rows, part] + here[:, part] * few[n, t : t + 1, part]
                if product is not None:
                    value = value + product[rows]
                staged[n, rows, part] = value.astype(BF)
        copy = pltpu.make_async_copy(staged.at[n], target, store_sem.at[n])
        copy.start()
        return copy

    few[0] = gathered(sent(0, HALF // 2))
    few[1] = gathered(sent(0, 0))
    store_dv = emit(0, dv_in, w_ref, gb, dv_hbm)
    store_dk = emit(1, dk_in, ds_ref, qb, dk_hbm)
    own = [
        tn(ds_ref[:, n * half : (n + 1) * half], k_ref[:, n * lanes : (n + 1) * lanes])
        for n in range(2)
    ]

    def own_piece(h, n):
        side = h * STEP // half
        block = own[side][h * STEP - side * half : (h + 1) * STEP - side * half]
        block = block[:, n * HALF - side * lanes : (n + 1) * HALF - side * lanes]
        return block + sent(1, 0)(h, n)

    few[2] = gathered(own_piece)
    store_dq = emit(2, dq_in, None, None, dq_hbm)
    store_dv.wait()
    store_dk.wait()
    store_dq.wait()


def in_hbm(x):
    return pltpu.with_memory_space_constraint(x, pltpu.MemorySpace.HBM)


def shards(queries, keys, values, grad_out, local_span, head_residue, valid_count):
    tokens, width = queries.shape
    heads = local_span.shape[0]
    chosen = heads * (tokens // STEP)
    assert heads == WINDOW and chosen == tokens
    vmem = pl.BlockSpec(memory_space=pltpu.VMEM)
    hbm = pl.BlockSpec(memory_space=pltpu.MemorySpace.HBM)
    out = jax.ShapeDtypeStruct((tokens, width), BF)
    full = pltpu.VMEM((tokens, width), F32)
    passed = pl.pallas_call(
        kernel,
        out_shape=(full, full, full)
        + (
            pltpu.VMEM((chosen, chosen), BF),
            pltpu.VMEM((tokens, chosen), F32),
            pltpu.VMEM((tokens, chosen), F32),
            pltpu.VMEM((width, chosen), BF),
            pltpu.VMEM((width, chosen), BF),
            pltpu.VMEM((tokens, width), BF),
            pltpu.VMEM((STEP, width), F32),
        ),
        in_specs=[hbm] * 7,
        out_specs=(vmem,) * 10,
        scratch_shapes=[pltpu.VMEM((tokens, width), BF)] * 3
        + [pltpu.SemaphoreType.DMA((4,))]
        + [pltpu.VMEM((width, tokens), BF)] * 4
        + [pltpu.VMEM((width, tokens), F32)] * 3
        + [
            pltpu.VMEM((tokens, chosen), BF),
            pltpu.VMEM((tokens, tokens), jnp.int32),
            pltpu.VMEM((2, tokens, tokens), BF),
            pltpu.VMEM((2, tokens, tokens), BF),
        ]
        + [pltpu.VMEM((chosen, chosen), BF)] * 3
        + [pltpu.SemaphoreType.DMA] * 4
        + [pltpu.SMEM((heads,), jnp.int32)] * 2
        + [pltpu.SMEM((1,), jnp.int32), pltpu.SemaphoreType.DMA((3,))],
        compiler_params=pltpu.CompilerParams(
            collective_id=0, has_side_effects=True, vmem_limit_bytes=VMEM_LIMIT
        ),
    )(
        *[in_hbm(x) for x in (local_span, head_residue)],
        valid_count,
        *[in_hbm(x) for x in (queries, keys, values, grad_out)],
    )
    return pl.pallas_call(
        finish,
        out_shape=(out, out, out),
        in_specs=[vmem] * 10,
        out_specs=(hbm, hbm, hbm),
        scratch_shapes=[
            pltpu.VMEM((3, tokens, width), BF),
            pltpu.VMEM((3, STEP, width), F32),
            pltpu.VMEM((tokens, chosen), BF),
            pltpu.VMEM((tokens, chosen), BF),
            pltpu.SemaphoreType.DMA((3,)),
        ],
        compiler_params=pltpu.CompilerParams(vmem_limit_bytes=VMEM_LIMIT),
    )(*[pltpu.with_memory_space_constraint(x, pltpu.MemorySpace.VMEM) for x in passed])


def solution(mesh):
    rows = P(("groups", "seq"), None)
    return jax.shard_map(
        shards,
        mesh=mesh,
        in_specs=(rows, rows, rows, rows, P(), P(), P("groups")),
        out_specs=(rows, rows, rows),
        check_vma=False,
    )
```

```python
import math

import jax
import jax.numpy as jnp
from jax import lax
from jax.experimental import pallas as pl
from jax.experimental.pallas import tpu as pltpu
from jax.sharding import PartitionSpec as P

STEP = 16
WINDOW = 16
FIRST = (14, 12, 10, 8, 15, 13, 11, 9, 0, 2, 4, 6, 1, 3, 5, 7)
SECOND = (0, 1, 14, 12, 10, 8, 15, 13, 11, 9, 2, 4, 6, 3, 5, 7)
HALF = 128
FLOOR = -1e30
LOG2E = 1.4426950408889634
EARLY_HEADS = 10
VMEM_LIMIT = 48 * 2**20

BF = jnp.bfloat16
F32 = jnp.float32


def nn(a, b):
    return lax.dot_general(a, b, (((1,), (0,)), ((), ())), preferred_element_type=F32)


def nt(a, b):
    return lax.dot_general(a, b, (((1,), (1,)), ((), ())), preferred_element_type=F32)


def tn(a, b):
    return lax.dot_general(a, b, (((0,), (0,)), ((), ())), preferred_element_type=F32)


def parts_of(x, count):
    out = []
    for _ in range(count - 1):
        head = x.astype(BF).astype(F32)
        out.append(head)
        x = x - head
    out.append(x)
    return out


def rows_block(rows, height, width):
    at = lax.broadcasted_iota(jnp.int32, (height, width), 0)
    block = jnp.zeros((height, width), F32)
    for n, row in enumerate(rows):
        block = jnp.where(at == n, row, block)
    return block


def gather_rows(at, *counts):
    row = lax.broadcasted_iota(jnp.int32, (16, HALF), 0)
    lane = lax.broadcasted_iota(jnp.int32, (16, HALF), 1)
    total = jnp.zeros((16, HALF), F32)
    for n, count in enumerate(counts):
        hit = (row == n) & (lane >= at) & (lane < at + count)
        total = jnp.where(hit, 1.0, total)
        at += count
    return total.astype(BF)


def kernel(
    span_hbm, res_hbm, count_hbm, q_hbm, k_hbm, v_hbm, g_hbm,
    dq_ref, dk_ref, dv_ref, back_ref, pb, dpb, qb, gb, k_ref, here_ref,
    q_ref, v_ref, g_ref, load_sem, qt, kt, vt, gt, dqt, dkt, dvt, pick, far, w_ref, ds_ref,
    send1, recv1, send2, ss1, rs1, ss2, rs2, span_ref, res_ref, count_ref, small_sem,
):
    tokens, width = q_ref.shape
    heads = span_hbm.shape[0]
    dim = width // heads
    few = tokens // STEP
    chosen = heads * few
    scale = 1.0 / math.sqrt(dim)
    scale2 = scale * LOG2E
    me = lax.axis_index("seq")
    base = (me // WINDOW) * WINDOW
    my = me - base
    barrier = pltpu.get_barrier_semaphore()
    bits = [lax.rem(my // b, 2) for b in (1, 2, 4, 8)]
    for n in range(WINDOW - 1, 0, -1):
        to = my
        for at, b in enumerate((1, 2, 4, 8)):
            if n & b:
                to = to + b - 2 * b * bits[at]
        pl.semaphore_signal(
            barrier, inc=1, device_id={"seq": base + to},
            device_id_type=pl.DeviceIdType.MESH,
        )

    smalls = [
        pltpu.make_async_copy(source, target, small_sem.at[n])
        for n, (source, target) in enumerate(
            ((count_hbm, count_ref), (span_hbm, span_ref), (res_hbm, res_ref))
        )
    ]
    for small in smalls:
        small.start()
    loads = [
        pltpu.make_async_copy(source, target, load_sem.at[n])
        for n, (source, target) in enumerate(
            ((q_hbm, q_ref), (g_hbm, g_ref), (k_hbm, k_ref), (v_hbm, v_ref))
        )
    ]
    for load in loads:
        load.start()

    def block_of(n):
        return pl.ds(pl.multiple_of(n * few, few), few)

    def send_to(to, source, target, send_sem, recv_sem):
        return pltpu.make_async_remote_copy(
            src_ref=source.at[pl.ds(to * few, few)],
            dst_ref=target.at[block_of(my)],
            send_sem=send_sem,
            recv_sem=recv_sem,
            device_id={"seq": base + to},
            device_id_type=pl.DeviceIdType.MESH,
        )

    def start_all(order, *args):
        for to in order:
            @pl.when(my != to)
            def _():
                send_to(to, *args).start()

    def all_of(source, target, send_sem, recv_sem):
        others = pl.ds(0, (WINDOW - 1) * few)
        return pltpu.make_async_remote_copy(
            src_ref=source.at[others],
            dst_ref=target.at[others],
            send_sem=send_sem,
            recv_sem=recv_sem,
            device_id={"seq": base + lax.rem(my + 1, WINDOW)},
            device_id_type=pl.DeviceIdType.MESH,
        )

    def wait_all(*args):
        all_of(*args).wait_recv()

    def wait_sent(*args):
        all_of(*args).wait_send()

    for small in smalls:
        small.wait()
    count = count_ref[0]
    lane = lax.broadcasted_iota(jnp.int32, (1, chosen), 1)
    lane_head = lane // few
    lane_res = jnp.zeros((1, chosen), jnp.int32)
    lane_span = jnp.zeros((1, chosen), jnp.int32)
    for h in range(heads):
        lane_res = jnp.where(lane_head == h, res_ref[h], lane_res)
        lane_span = jnp.where(lane_head == h, span_ref[h], lane_span)
    lane_token = (lane % few) * STEP + lane_res
    row = lax.broadcasted_iota(jnp.int32, (tokens, tokens), 0)
    col = lax.broadcasted_iota(jnp.int32, (tokens, tokens), 1)
    start = me * tokens
    huge = jnp.int32(1 << 20)
    row_ok = row + start < count
    far[...] = jnp.where(row_ok, row ^ col, huge)
    pick[...] = (row == lane_token).astype(F32).astype(BF)

    for load, source, target in zip(
        loads, (q_ref, g_ref, k_ref, v_ref), (qt, gt, kt, vt)
    ):
        load.wait()
        target[...] = source[...].T

    def picked(source, keep):
        full = nn(source[...], pick[...])
        total = jnp.zeros((dim, chosen), F32)
        for h in range(heads):
            part = jnp.where(lane_head == h, full[h * dim : (h + 1) * dim], 0.0)
            if keep is not None:
                keep[h * dim : (h + 1) * dim, :] = part.astype(BF)
            total = total + part
        return total

    q_few = picked(qt, qb)
    g_few = picked(gt, gb)
    k_few = picked(kt, None)
    v_few = picked(vt, None)

    mask = jnp.where(row_ok, row ^ lane_token, huge) < lane_span
    s = jnp.where(mask, nn(k_ref[...], qb[...]) * scale2, FLOOR)
    top = jnp.max(s, axis=0, keepdims=True)
    p = jnp.exp2(s - top)
    total = jnp.sum(p, axis=0, keepdims=True)
    p = p * (1.0 / total)
    dp = nn(v_ref[...], gb[...])
    local_lse = top + jnp.log(total) * LOG2E
    local_delta = jnp.sum(p * dp, axis=0, keepdims=True)
    pb[...] = p
    dpb[...] = dp
    gap = HALF // 2 - dim
    stats = rows_block(parts_of(local_lse, 3) + parts_of(local_delta, 2), gap, chosen)
    blank = jnp.zeros((gap, chosen), F32)
    packed = jnp.concatenate(
        [q_few, stats, v_few, blank, k_few, blank, g_few, blank], axis=0
    )
    send1[...] = packed.T.astype(BF)

    pl.semaphore_wait(barrier, WINDOW - 1)
    start_all(FIRST, send1, recv1, ss1, rs1)
    recv1[block_of(my), :] = send1[block_of(my), :]

    query_ok = lane + start < count

    def head_at(h):
        return pl.ds(pl.multiple_of(h * dim, 16), dim)

    def weigh(h, slot):
        at = head_at(h)
        qh, kh, vh, gh = qt[at, :], kt[at, :], vt[at, :], gt[at, :]
        s = jnp.where(far[...] < span_ref[h], tn(kh, qh) * scale2, FLOOR)
        top = jnp.max(s, axis=0, keepdims=True)
        p = jnp.exp2(s - top)
        inverse = 1.0 / jnp.sum(p, axis=0, keepdims=True)
        dp = tn(vh, gh)
        delta = jnp.sum(p * dp, axis=0, keepdims=True) * inverse
        keep = query_ok & (lane % STEP != res_ref[h])
        w = p * jnp.where(keep, inverse, 0.0)
        w_ref[slot] = w.astype(BF)
        ds_ref[slot] = (w * (dp - delta)).astype(BF)

    def gather(h, slot):
        at = head_at(h)
        dqt[at, :] = nn(kt[at, :], ds_ref[slot]) * scale
        dkt[at, :] = nt(qt[at, :], ds_ref[slot]) * scale
        dvt[at, :] = nt(gt[at, :], w_ref[slot])

    def local_heads(first, last):
        weigh(first, 0)
        weigh(first + 1, 1)

        def pair(n, carry):
            h = first + 2 * n
            gather(h - 2, 0)
            weigh(h, 0)
            gather(h - 1, 1)
            weigh(h + 1, 1)
            return carry

        lax.fori_loop(1, (last - first) // 2, pair, 0)
        gather(last - 2, 0)
        gather(last - 1, 1)

    local_heads(0, EARLY_HEADS)

    wait_all(send1, recv1, ss1, rs1)
    at = lax.broadcasted_iota(jnp.int32, (1, HALF), 1)
    low = at < HALF // 2
    first = jnp.where(at < dim, 1.0, 0.0).astype(BF)
    second = jnp.where((at >= HALF // 2) & (at < HALF // 2 + dim), 1.0, 0.0).astype(BF)
    left, right = recv1[:, :HALF], recv1[:, HALF:]
    limit = count - base * tokens - res_ref[my]
    rows_left = (limit + STEP - 1) // STEP
    s = jnp.where(row < rows_left, nt(right * first, left) * scale2, FLOOR)
    stats = nt(gather_rows(dim, 3, 2), left)
    local_lse, local_delta = stats[0:1], stats[1:2]
    dp = nt(left * second, right)
    top = jnp.max(s, axis=0, keepdims=True)
    p = jnp.exp2(s - top)
    total = jnp.sum(p, axis=0, keepdims=True)
    dilated_lse = top + jnp.log(total) * LOG2E
    most = jnp.maximum(local_lse, dilated_lse)
    both = most + jnp.log(jnp.exp2(local_lse - most) + jnp.exp2(dilated_lse - most)) * LOG2E
    here_ok = lane * STEP < limit
    local_part = jnp.where(here_ok, jnp.exp2(local_lse - both), 0.0)
    u = p * jnp.where(here_ok, jnp.exp2(top - both), 0.0)
    delta = local_part * local_delta + jnp.sum(u * dp, axis=0, keepdims=True)
    delta = jnp.where(here_ok, delta, 0.0)
    ds = (u * (dp - delta)).astype(BF)
    stats = rows_block(parts_of(local_part, 2) + parts_of(delta, 2), 16, chosen)
    dk_dv = jnp.where(low, nn(ds, left) * scale, nn(u.astype(BF), right))
    send2[:, :HALF] = dk_dv.astype(BF)
    place = lax.broadcasted_iota(jnp.int32, (16, HALF), 0) + HALF // 2
    place = (place == lax.broadcasted_iota(jnp.int32, (16, HALF), 1)).astype(F32)
    dq_stats = jnp.where(low, tn(ds, right) * scale, tn(stats.astype(BF), place.astype(BF)))
    send2[:, HALF:] = dq_stats.astype(BF)
    start_all(SECOND, send2, back_ref, ss2, rs2)
    back_ref[block_of(my), :] = send2[block_of(my), :]

    local_heads(EARLY_HEADS, heads)

    dq_ref[...] = dqt[...].T
    dk_ref[...] = dkt[...].T
    dv_ref[...] = dvt[...].T
    wide = lax.broadcasted_iota(jnp.int32, (STEP, width), 1)
    wide_res = jnp.zeros((STEP, width), jnp.int32)
    for h in range(heads):
        wide_res = jnp.where(wide >= h * dim, res_ref[h], wide_res)
    at = lax.broadcasted_iota(jnp.int32, (STEP, width), 0)
    here_ref[...] = (at == wide_res).astype(F32)

    wait_sent(send1, recv1, ss1, rs1)
    wait_all(send2, back_ref, ss2, rs2)
    wait_sent(send2, back_ref, ss2, rs2)


def finish(
    dq_in, dk_in, dv_in, back, pb, dpb, qb, gb, k_ref, here,
    dq_hbm, dk_hbm, dv_hbm, staged, few, ds_ref, w_ref, store_sem,
):
    tokens, width = dq_in.shape
    chosen = pb.shape[1]
    heads = chosen // STEP
    dim = width // heads
    scale = 1.0 / math.sqrt(dim)
    half, lanes = chosen // 2, width // 2
    stats = nt(gather_rows(HALF // 2, 2, 2), back[:, HALF:])
    w = pb[...] * stats[0:1]
    w_ref[...] = w.astype(BF)
    ds_ref[...] = (w * ((dpb[...] - stats[1:2]) * scale)).astype(BF)
    at = lax.broadcasted_iota(jnp.int32, (STEP, HALF), 1)

    def tiles_of(h):
        first = h * dim // HALF
        return range(first, (h * dim + dim - 1) // HALF + 1)

    def gathered(piece_of):
        tiles = [jnp.zeros((STEP, HALF), F32) for _ in range(width // HALF)]
        for h in range(heads):
            for n in tiles_of(h):
                start = h * dim - n * HALF
                here_too = (at >= start) & (at < start + dim)
                tiles[n] = jnp.where(here_too, piece_of(h, n), tiles[n])
        return jnp.concatenate(tiles, axis=1)

    def sent(column, start):
        def piece(h, n):
            block = back[h * STEP : (h + 1) * STEP, column * HALF : (column + 1) * HALF]
            return pltpu.roll(block.astype(F32), (h * dim - start) % HALF, axis=1)

        return piece

    def emit(n, source, factor, other, target):
        for start in range(0, width, chosen):
            part = slice(start, start + chosen)
            product = None if factor is None else nt(factor[...], other[part])
            for t in range(tokens // STEP):
                rows = slice(t * STEP, (t + 1) * STEP)
                value = source[rows, part] + here[:, part] * few[n, t : t + 1, part]
                if product is not None:
                    value = value + product[rows]
                staged[n, rows, part] = value.astype(BF)
        copy = pltpu.make_async_copy(staged.at[n], target, store_sem.at[n])
        copy.start()
        return copy

    few[0] = gathered(sent(0, HALF // 2))
    few[1] = gathered(sent(0, 0))
    store_dv = emit(0, dv_in, w_ref, gb, dv_hbm)
    store_dk = emit(1, dk_in, ds_ref, qb, dk_hbm)
    own = [
        tn(ds_ref[:, n * half : (n + 1) * half], k_ref[:, n * lanes : (n + 1) * lanes])
        for n in range(2)
    ]

    def own_piece(h, n):
        side = h * STEP // half
        block = own[side][h * STEP - side * half : (h + 1) * STEP - side * half]
        block = block[:, n * HALF - side * lanes : (n + 1) * HALF - side * lanes]
        return block + sent(1, 0)(h, n)

    few[2] = gathered(own_piece)
    store_dq = emit(2, dq_in, None, None, dq_hbm)
    store_dv.wait()
    store_dk.wait()
    store_dq.wait()


def in_hbm(x):
    return pltpu.with_memory_space_constraint(x, pltpu.MemorySpace.HBM)


def shards(queries, keys, values, grad_out, local_span, head_residue, valid_count):
    tokens, width = queries.shape
    heads = local_span.shape[0]
    chosen = heads * (tokens // STEP)
    assert heads == WINDOW and chosen == tokens
    vmem = pl.BlockSpec(memory_space=pltpu.VMEM)
    hbm = pl.BlockSpec(memory_space=pltpu.MemorySpace.HBM)
    out = jax.ShapeDtypeStruct((tokens, width), BF)
    full = pltpu.VMEM((tokens, width), F32)
    passed = pl.pallas_call(
        kernel,
        out_shape=(full, full, full)
        + (
            pltpu.VMEM((chosen, chosen), BF),
            pltpu.VMEM((tokens, chosen), F32),
            pltpu.VMEM((tokens, chosen), F32),
            pltpu.VMEM((width, chosen), BF),
            pltpu.VMEM((width, chosen), BF),
            pltpu.VMEM((tokens, width), BF),
            pltpu.VMEM((STEP, width), F32),
        ),
        in_specs=[hbm] * 7,
        out_specs=(vmem,) * 10,
        scratch_shapes=[pltpu.VMEM((tokens, width), BF)] * 3
        + [pltpu.SemaphoreType.DMA((4,))]
        + [pltpu.VMEM((width, tokens), BF)] * 4
        + [pltpu.VMEM((width, tokens), F32)] * 3
        + [
            pltpu.VMEM((tokens, chosen), BF),
            pltpu.VMEM((tokens, tokens), jnp.int32),
            pltpu.VMEM((2, tokens, tokens), BF),
            pltpu.VMEM((2, tokens, tokens), BF),
        ]
        + [pltpu.VMEM((chosen, chosen), BF)] * 3
        + [pltpu.SemaphoreType.DMA] * 4
        + [pltpu.SMEM((heads,), jnp.int32)] * 2
        + [pltpu.SMEM((1,), jnp.int32), pltpu.SemaphoreType.DMA((3,))],
        compiler_params=pltpu.CompilerParams(
            collective_id=0, has_side_effects=True, vmem_limit_bytes=VMEM_LIMIT
        ),
    )(
        *[in_hbm(x) for x in (local_span, head_residue)],
        valid_count,
        *[in_hbm(x) for x in (queries, keys, values, grad_out)],
    )
    return pl.pallas_call(
        finish,
        out_shape=(out, out, out),
        in_specs=[vmem] * 10,
        out_specs=(hbm, hbm, hbm),
        scratch_shapes=[
            pltpu.VMEM((3, tokens, width), BF),
            pltpu.VMEM((3, STEP, width), F32),
            pltpu.VMEM((tokens, chosen), BF),
            pltpu.VMEM((tokens, chosen), BF),
            pltpu.SemaphoreType.DMA((3,)),
        ],
        compiler_params=pltpu.CompilerParams(vmem_limit_bytes=VMEM_LIMIT),
    )(*[pltpu.with_memory_space_constraint(x, pltpu.MemorySpace.VMEM) for x in passed])


def solution(mesh):
    rows = P(("groups", "seq"), None)
    return jax.shard_map(
        shards,
        mesh=mesh,
        in_specs=(rows, rows, rows, rows, P(), P(), P("groups")),
        out_specs=(rows, rows, rows),
        check_vma=False,
    )
```
